32 devices in a mesh: groups: 2 (over x), pool: 2 (over core), tensor: 8 (over z, y).
Axes of the slice: x: 2, y: 2, z: 4, core: 2. Of those that a mesh axis runs over, the one named last changes fastest.
Arguments:
- rows: bfloat16 [512, 8192], P(('groups', 'pool', 'tensor')), parts along dimension 0, may hold values from -6 to 6
- norm_gain: float32 [8192], replicated, may hold values from 0.1 to 1.9
- w_query: bfloat16 [8192, 8192], P(None, ('pool', 'tensor')), may hold values from -0.0625 to 0.0625
- w_keyval: bfloat16 [8192, 2048], P(None, ('pool', 'tensor')), may hold values from -0.125 to 0.125
- w_out: bfloat16 [8192, 8192], P(('pool', 'tensor')), may hold values from -0.25 to 0.25
- key_cache: bfloat16 [512, 256, 1024], P(('groups', 'pool', 'tensor')), parts along dimension 0, may hold values from -104 to 104
- value_cache: bfloat16 [512, 256, 1024], P(('groups', 'pool', 'tensor')), parts along dimension 0, may hold values from -6 to 6
- lengths: int32 [512], P('groups'), parts along dimension 0, may hold values from 1 to 256, as said below
- slot_of: int32 [512], P('groups'), parts along dimension 0, may hold values from 0 to 255, each once
Outputs:
- projected: bfloat16 [512, 8192], P(('groups', 'pool', 'tensor')), parts along dimension 0
The draws below stay inside these ranges and needn't reach their ends.
There are 2 independent parts, one for each index of `groups`. The reference program is written for one: setup_inputs(seed, part) draws one part's arguments, and reference() takes and returns one part's arrays. A program takes and returns all parts, laid end to end along the dimension named above; an argument that names none is the same for every part. Nothing has to cross between parts.
Inputs may be any that keep to these rules, and one draw needn't show every extreme that they name: `slot_of`: slots 16 * i to 16 * (i + 1) - 1 lie on index i of pool+tensor; every slot belongs to exactly one request. `lengths`: some request has exactly 256 cached tokens.
All inputs are finite; a program needn't handle non-finite values.
Results may differ from the reference program's by a relative error of at most 0.024.
Values may be sent and summed in bfloat16 or wider, within the bound.
No kernel may reach another device: no remote copies, remote signals or barrier semaphores. Data moves between devices by JAX's collectives and lax.ppermute only.
A program may use at most 128 MiB of HBM per device.

```python
import jax
import jax.numpy as jnp
from jax import lax

D = 8192
HEADS = 64
KVH = 8
HD = 128
L = 256
REQUESTS = 256
N_POOL = 2
N_TENSOR = 8


def draw_lengths(key, part):
    key_top = jax.random.fold_in(key, 11)
    key_val = jax.random.fold_in(key, 12)
    key_pick = jax.random.fold_in(key, 13)
    upper = jax.random.randint(key_top, (REQUESTS,), 1, L + 1)
    raw = jax.random.randint(key_val, (REQUESTS,), 0, L)
    values = raw % upper + 1
    chosen = jax.random.randint(key_pick, (), 0, REQUESTS)
    return jnp.where(jnp.arange(REQUESTS) == chosen, L, values).astype(jnp.int32)


def draw_key_cache(key, part):
    base = jax.random.fold_in(key, 21)
    values = jnp.clip(2.0 * jax.random.normal(jax.random.fold_in(base, 5), (REQUESTS, L, KVH, HD), jnp.float32), -12.0, 12.0)
    return values.reshape(REQUESTS, L, KVH * HD).astype(jnp.bfloat16)


def shard_levels(key, dims, shards, low, high):
    loudness, own = 1.0, jax.random.fold_in(key, 6)
    for position, shards_of in shards:
        draws = jnp.exp(jax.random.uniform(jax.random.fold_in(own, position), (shards_of,), jnp.float32, low / len(shards), high / len(shards)))
        loudness = loudness * jnp.repeat(draws, dims[position] // shards_of).reshape([-1 if axis == position else 1 for axis in range(len(dims))])
    return loudness


def centred(own_key, dims, width, most, shards=(), held_as=jnp.bfloat16):
    entries = jax.random.normal(own_key, dims, jnp.float32) * width
    if len(shards) > 0:
        entries = shard_levels(own_key, dims, shards, -0.22, 0.18) * entries
    return jnp.clip(entries, min=-most, max=most).astype(held_as)


def setup_inputs(seed: int = 0, part: int = 0) -> dict:
    key_list = jax.random.split(jax.random.key(seed), 10)
    own_keys = jax.random.split(jax.random.fold_in(key_list[9], part), 10)
    rows = centred(own_keys[0], (REQUESTS, D), 1.0, 6.0, ((0, 16),))
    norm_gain = jnp.clip(1.0 + 0.18 * jax.random.normal(key_list[1], (D,), jnp.float32), 0.1, 1.9)
    w_query = centred(key_list[2], (D, HEADS * HD), D ** -0.5, 0.0625, ((1, 16),))
    w_keyval = centred(key_list[3], (D, 2 * KVH * HD), (D // 4) ** -0.5, 0.125, ((1, 16),))
    w_out = centred(key_list[4], (HEADS * HD, D), (HEADS * HD // 16) ** -0.5, 0.25, ((0, 16),))
    key_cache = draw_key_cache(jax.random.fold_in(jax.random.fold_in(key_list[9], part), 71), part)
    value_cache = centred(own_keys[6], (REQUESTS, L, KVH * HD), 1.0, 6.0, ((0, 16),))
    lengths = draw_lengths(jax.random.fold_in(jax.random.fold_in(key_list[9], part), 71), part)
    slot_of = jax.random.permutation(own_keys[8], REQUESTS).astype(jnp.int32)
    return dict(rows=rows, norm_gain=norm_gain, w_query=w_query, w_keyval=w_keyval, w_out=w_out, key_cache=key_cache, value_cache=value_cache, lengths=lengths, slot_of=slot_of)


EPS = 1e-05

def reference(rows, norm_gain, w_query, w_keyval, w_out, key_cache, value_cache, lengths, slot_of):
    values32 = rows.astype(jnp.float32)
    normed = (values32 * lax.rsqrt(lax.optimization_barrier(jnp.mean(values32 * values32, axis=1, keepdims=True)) + EPS) * norm_gain.astype(jnp.float32)).astype(jnp.bfloat16)
    queries = jnp.dot(normed, w_query, preferred_element_type=jnp.float32).astype(jnp.bfloat16)
    keyvals = jnp.dot(normed, w_keyval, preferred_element_type=jnp.float32).astype(jnp.bfloat16)
    group = HEADS // KVH
    positions = jnp.arange(L, dtype=jnp.int32)
    scale = HD ** (-0.5)

    def attend(inputs):
        query, keyval, slot, length = inputs
        cached_keys = lax.dynamic_index_in_dim(key_cache, slot, 0, keepdims=False).astype(jnp.float32).reshape(L, KVH, HD)
        cached_values = lax.dynamic_index_in_dim(value_cache, slot, 0, keepdims=False).astype(jnp.float32).reshape(L, KVH, HD)
        heads = query.astype(jnp.float32).reshape(KVH, group, HD)
        new_key = keyval[:KVH * HD].astype(jnp.float32).reshape(KVH, HD)
        new_value = keyval[KVH * HD:].astype(jnp.float32).reshape(KVH, HD)
        scores = jnp.einsum('kgd,lkd->kgl', heads, cached_keys) * scale
        scores = jnp.where((positions < length)[None, None, :], scores, -1e+30)
        own = jnp.einsum('kgd,kd->kg', heads, new_key) * scale
        top = jnp.maximum(lax.optimization_barrier(jnp.max(scores, axis=2)), own)
        probs = jnp.exp(scores - top[..., None])
        own_prob = jnp.exp(own - top)
        totals = lax.optimization_barrier(jnp.sum(probs, axis=2)) + own_prob
        probs_low = lax.optimization_barrier(probs.astype(jnp.bfloat16)).astype(jnp.float32)
        own_low = lax.optimization_barrier(own_prob.astype(jnp.bfloat16)).astype(jnp.float32)
        weighted = jnp.einsum('kgl,lkd->kgd', probs_low, cached_values) + own_low[..., None] * new_value[:, None, :]
        return (weighted / totals[..., None]).astype(jnp.bfloat16).reshape(HEADS * HD)
    attended = lax.map(attend, (queries, keyvals, slot_of.astype(jnp.int32), lengths.astype(jnp.int32)))
    pieces = N_POOL * N_TENSOR
    piece = HEADS * HD // pieces
    att_parts = attended.reshape(REQUESTS, pieces, piece)
    weight_parts = w_out.reshape(pieces, piece, D)

    def add_part(total, index):
        part_att = lax.dynamic_index_in_dim(att_parts, index, 1, keepdims=False)
        part_weight = lax.dynamic_index_in_dim(weight_parts, index, 0, keepdims=False)
        term = jnp.dot(part_att, part_weight, preferred_element_type=jnp.float32)
        term = lax.optimization_barrier(term.astype(jnp.bfloat16)).astype(jnp.float32)
        return (total + term, None)
    summed, _ = lax.scan(add_part, jnp.zeros((REQUESTS, D), jnp.float32), jnp.arange(pieces, dtype=jnp.int32))
    return summed.astype(jnp.bfloat16)
```

```python
import jax
import jax.numpy as jnp
from jax import lax
from jax.experimental import pallas as pl
from jax.experimental.pallas import tpu as pltpu
from jax.sharding import PartitionSpec as P

HEADS = 64
KVH = 8
HD = 128
EPS = 1e-05
AXES = ("pool", "tensor")
MIB = 1 << 20


def ring_order(size):
    return list(range(0, size, 2)) + list(range(size - 1, 0, -2))


def ring_pairs(size):
    ring = ring_order(size)
    return [
        (p * size + ring[k], p * size + ring[(k + 1 - 2 * p) % size])
        for p in range(2)
        for k in range(size)
    ]


def sibling_pairs(size):
    return [(p * size + t, (1 - p) * size + t) for p in range(2) for t in range(size)]


def project_kernel(count, *refs):
    blocks = refs[:count]
    slots_ref, wq_ref, wkv_ref, out_ref, rows, acc, sems = refs[count:]
    step = pl.program_id(0)
    block_rows = blocks[0].shape[0]
    depth = wq_ref.shape[0]
    query_cols = wq_ref.shape[1]

    @pl.when(step == 0)
    def _():
        copies = [
            pltpu.make_async_copy(b, rows.at[pl.ds(i * block_rows, block_rows)], sems.at[i])
            for i, b in enumerate(blocks)
        ]
        for copy in copies:
            copy.start()
        acc[...] = jnp.zeros_like(acc)
        for copy in copies:
            copy.wait()

    part = rows[:, pl.ds(pl.multiple_of(step * depth, depth), depth)]
    acc[:, :query_cols] += jnp.dot(part, wq_ref[...], preferred_element_type=jnp.float32)
    acc[:, query_cols:] += jnp.dot(part, wkv_ref[...], preferred_element_type=jnp.float32)

    @pl.when(step == pl.num_programs(0) - 1)
    def _():
        requests = rows.shape[0]
        ids = lax.broadcasted_iota(jnp.int32, (requests, requests), 0)
        order = (slots_ref[...] == ids).astype(jnp.bfloat16)
        out_ref[...] = jnp.dot(
            order, acc[...].astype(jnp.bfloat16), preferred_element_type=jnp.float32
        ).astype(jnp.bfloat16)


def project(blocks, slots_local, w_query, w_keyval, depth):
    count = len(blocks)
    model = blocks[0].shape[1]
    requests = blocks[0].shape[0] * count
    width = w_query.shape[1] + w_keyval.shape[1]
    any_spec = pl.BlockSpec(memory_space=pl.ANY)
    return pl.pallas_call(
        lambda *refs: project_kernel(count, *refs),
        grid=(model // depth,),
        in_specs=[any_spec] * count
        + [
            pl.BlockSpec((1, requests), lambda i: (0, 0)),
            pl.BlockSpec((depth, w_query.shape[1]), lambda i: (i, 0)),
            pl.BlockSpec((depth, w_keyval.shape[1]), lambda i: (i, 0)),
        ],
        out_specs=pl.BlockSpec((requests, width), lambda i: (0, 0)),
        out_shape=jax.ShapeDtypeStruct((requests, width), jnp.bfloat16),
        scratch_shapes=[
            pltpu.VMEM((requests, model), jnp.bfloat16),
            pltpu.VMEM((requests, width), jnp.float32),
            pltpu.SemaphoreType.DMA((count,)),
        ],
        compiler_params=pltpu.CompilerParams(vmem_limit_bytes=24 * MIB),
        name="project",
    )(*blocks, slots_local.reshape(1, requests), w_query, w_keyval)


def attend_kernel(query_cols, len_ref, arrived_ref, keys_ref, values_ref, out_ref,
                  full, scores, probs, weights, packed):
    slots = keys_ref.shape[0]
    cached = keys_ref.shape[1]
    kv_width = keys_ref.shape[2]
    devices = arrived_ref.shape[0] // slots
    per_dev = query_cols // HD
    kv_cols = arrived_ref.shape[1] - query_cols
    pieces = HD // kv_cols
    group = HEADS // KVH
    scale = HD ** (-0.5)
    for i in range(per_dev):
        full[i] = arrived_ref[:, i * HD : (i + 1) * HD].astype(jnp.float32)
    full[per_dev, :, :kv_cols] = arrived_ref[:, query_cols:].astype(jnp.float32)
    row = lax.broadcasted_iota(jnp.int32, (HEADS, 1), 0)
    kv_head = ((row % devices) * per_dev + row // devices) // group
    lane_head = lax.broadcasted_iota(jnp.int32, (HEADS, kv_width), 1) // HD
    block_mask = lane_head == kv_head
    dev_head = (lax.broadcasted_iota(jnp.int32, (devices, devices), 0) * per_dev) // group
    source = lax.broadcasted_iota(jnp.int32, (devices, devices), 1)
    position = lax.broadcasted_iota(jnp.int32, (HEADS, cached), 1)

    def of_slot(s, i):
        return full[i, pl.ds(s, devices, stride=slots), :]

    def new_rows(s, first):
        cut = of_slot(s, per_dev)[:, :kv_cols]
        parts = []
        for i in range(pieces):
            pick = (source == first + dev_head * pieces + i).astype(jnp.float32)
            parts.append(
                jnp.dot(pick, cut, preferred_element_type=jnp.float32, precision=lax.Precision.HIGHEST)
            )
        one = parts[0] if pieces == 1 else jnp.concatenate(parts, axis=1)
        return jnp.concatenate([one] * per_dev, axis=0)

    owns = []
    for s in range(slots):
        q = jnp.concatenate([of_slot(s, i) for i in range(per_dev)], axis=0)
        wide = jnp.where(block_mask, jnp.concatenate([q] * KVH, axis=1), 0.0).astype(jnp.bfloat16)
        scores[s] = lax.dot_general(
            wide, keys_ref[s], (((1,), (1,)), ((), ())), preferred_element_type=jnp.float32
        )
        owns.append(jnp.sum(q * new_rows(s, 0), axis=1, keepdims=True) * scale)
    for s in range(slots):
        sc = jnp.where(position < len_ref[s], scores[s] * scale, -1e30)
        top = jnp.maximum(jnp.max(sc, axis=1, keepdims=True), owns[s])
        pr = jnp.exp(sc - top)
        own_prob = jnp.exp(owns[s] - top)
        total = jnp.sum(pr, axis=1, keepdims=True) + own_prob
        probs[s] = pr.astype(jnp.bfloat16)
        own_low = own_prob.astype(jnp.bfloat16).astype(jnp.float32)
        weights[s] = jnp.concatenate([own_low, total], axis=1)
    for s in range(slots):
        all_heads = jnp.dot(probs[s], values_ref[s], preferred_element_type=jnp.float32)
        mine = jnp.zeros((HEADS, HD), jnp.float32)
        for k in range(KVH):
            mine = jnp.where(kv_head == k, all_heads[:, k * HD : (k + 1) * HD], mine)
        wt = weights[s]
        mine = (mine + wt[:, 0:1] * new_rows(s, devices // 2)) / wt[:, 1:2]
        for i in range(per_dev):
            packed[i, pl.ds(s, devices, stride=slots), :] = mine[i * devices : (i + 1) * devices]
    for i in range(per_dev):
        out_ref[:, i * HD : (i + 1) * HD] = packed[i].astype(jnp.bfloat16)


def attend(slot_len, arrived, key_cache, value_cache, query_cols):
    slots, cached, _ = key_cache.shape
    rows = arrived.shape[0]
    whole = pl.BlockSpec(memory_space=pltpu.VMEM)
    return pl.pallas_call(
        lambda *refs: attend_kernel(query_cols, *refs),
        in_specs=[pl.BlockSpec(memory_space=pltpu.SMEM), whole, whole, whole],
        out_specs=whole,
        out_shape=jax.ShapeDtypeStruct((rows, query_cols), jnp.bfloat16),
        scratch_shapes=[
            pltpu.VMEM((query_cols // HD + 1, rows, HD), jnp.float32),
            pltpu.VMEM((slots, HEADS, cached), jnp.float32),
            pltpu.VMEM((slots, HEADS, cached), jnp.bfloat16),
            pltpu.VMEM((slots, HEADS, 2), jnp.float32),
            pltpu.VMEM((query_cols // HD, rows, HD), jnp.float32),
        ],
        compiler_params=pltpu.CompilerParams(vmem_limit_bytes=40 * MIB),
        name="attend",
    )(slot_len, arrived, key_cache, value_cache)


def output_kernel(slots_ref, back_ref, w_ref, other_ref, mine_ref, rows):
    requests = back_ref.shape[0]

    @pl.when(pl.program_id(0) == 0)
    def _():
        ids = lax.broadcasted_iota(jnp.int32, (requests, requests), 1)
        order = (slots_ref[...] == ids).astype(jnp.bfloat16)
        rows[...] = jnp.dot(
            order, back_ref[...], preferred_element_type=jnp.float32
        ).astype(jnp.bfloat16)

    out = jnp.dot(rows[...], w_ref[...], preferred_element_type=jnp.float32).astype(jnp.bfloat16)
    other_ref[...] = out[: requests // 2]
    mine_ref[...] = out[requests // 2 :]


def output(slots_local, returned, w_out, cols):
    requests, depth = returned.shape
    model = w_out.shape[1]
    half = jax.ShapeDtypeStruct((requests // 2, model), jnp.bfloat16)
    half_spec = pl.BlockSpec((requests // 2, cols), lambda i: (0, i))
    return pl.pallas_call(
        output_kernel,
        grid=(model // cols,),
        in_specs=[
            pl.BlockSpec((requests, 1), lambda i: (0, 0)),
            pl.BlockSpec((requests, depth), lambda i: (0, 0)),
            pl.BlockSpec((depth, cols), lambda i: (0, i)),
        ],
        out_specs=[half_spec, half_spec],
        out_shape=[half, half],
        scratch_shapes=[pltpu.VMEM((requests, depth), jnp.bfloat16)],
        compiler_params=pltpu.CompilerParams(vmem_limit_bytes=24 * MIB),
        name="output",
    )(slots_local.reshape(requests, 1), returned, w_out)


def body(rows, norm_gain, w_query, w_keyval, w_out, key_cache, value_cache, lengths, slot_of):
    size = lax.axis_size("tensor")
    devices = lax.axis_size(AXES)
    half = size // 2
    block = rows.shape[0]
    slots_dev = key_cache.shape[0]
    query_cols = w_query.shape[1]
    forward = lambda x: lax.ppermute(x, AXES, ring_pairs(size))
    swap = lambda x: lax.ppermute(x, AXES, sibling_pairs(size))

    pool = lax.axis_index("pool")
    tensor = lax.axis_index("tensor")
    way = 1 - 2 * pool
    place = jnp.where(tensor % 2 == 0, tensor // 2, size - 1 - tensor // 2)

    def device_at(steps, owner):
        at = (place + way * steps + 2 * size) % size
        return owner * size + jnp.where(at < half, 2 * at, 2 * (size - 1 - at) + 1)

    slot_blocks = slot_of.reshape(devices, block)

    def slots_in(order):
        pick = jnp.stack(order)[:, None] == jnp.arange(devices, dtype=jnp.int32)[None, :]
        return jnp.sum(jnp.where(pick[:, :, None], slot_blocks[None], 0), axis=1).reshape(-1)

    values32 = rows.astype(jnp.float32)
    normed = (
        values32 * lax.rsqrt(jnp.mean(values32 * values32, axis=1, keepdims=True) + EPS) * norm_gain
    ).astype(jnp.bfloat16)
    a, b = lax.optimization_barrier((normed, swap(normed)))
    blocks, order = [a, b], [device_at(0, pool), device_at(0, 1 - pool)]
    for k in range(1, half):
        a, b = forward(a), forward(b)
        blocks += [a, b, swap(a), swap(b)]
        order += [
            device_at(-k, pool),
            device_at(-k, 1 - pool),
            device_at(k, 1 - pool),
            device_at(k, pool),
        ]
    a = forward(a)
    blocks += [a, swap(a)]
    order += [device_at(-half, pool), device_at(half, 1 - pool)]

    sending = project(blocks, slots_in(order), w_query, w_keyval, w_query.shape[0] // 8)
    arrived = lax.all_to_all(sending, AXES, split_axis=0, concat_axis=0, tiled=True)

    own_slots = lax.axis_index(AXES) * slots_dev + jnp.arange(slots_dev, dtype=jnp.int32)
    slot_len = jnp.sum(
        jnp.where(slot_of[None, :] == own_slots[:, None], lengths[None, :], 0), axis=1
    )
    attended = attend(slot_len, arrived, key_cache, value_cache, query_cols)
    returned = lax.all_to_all(attended, AXES, split_axis=0, concat_axis=0, tiled=True)

    theirs, mine = [device_at(-half, 1 - pool)], [device_at(half, pool)]
    for k in range(half - 1, 0, -1):
        theirs += [device_at(-k, 1 - pool), device_at(-k, pool)]
        mine += [device_at(k, pool), device_at(k, 1 - pool)]
    theirs += [device_at(0, 1 - pool)]
    mine += [device_at(0, pool)]
    other, own = output(slots_in(theirs + mine), returned, w_out, w_out.shape[1] // 8)
    got = swap(other)

    def chip_sum(i):
        cut = slice(i * block, (i + 1) * block)
        return own[cut].astype(jnp.float32) + got[cut].astype(jnp.float32)

    low = lambda x: x.astype(jnp.bfloat16)
    a, b = lax.optimization_barrier((low(chip_sum(0)), low(chip_sum(2))))
    a, b = forward(a), forward(b)
    at = 1
    for k in range(half - 1, 0, -1):
        a = forward(low(chip_sum(at) + a.astype(jnp.float32)))
        if k > 1:
            b = forward(low(chip_sum(at + 3) + b.astype(jnp.float32)))
        at += 2
    across = swap(b)
    return low(chip_sum(at) + a.astype(jnp.float32) + across.astype(jnp.float32))


def solution(mesh):
    placed = (
        P(("groups", "pool", "tensor"), None),
        P(),
        P(None, ("pool", "tensor")),
        P(None, ("pool", "tensor")),
        P(("pool", "tensor"), None),
        P(("groups", "pool", "tensor"), None, None),
        P(("groups", "pool", "tensor"), None, None),
        P("groups"),
        P("groups"),
    )
    return jax.shard_map(
        body,
        mesh=mesh,
        in_specs=placed,
        out_specs=P(("groups", "pool", "tensor"), None),
        check_vma=False,
    )
```

```python
import jax
import jax.numpy as jnp
from jax import lax
from jax.experimental import pallas as pl
from jax.experimental.pallas import tpu as pltpu
from jax.sharding import PartitionSpec as P


HEADS = 64
KVH = 8
HD = 128
EPS = 1e-05
AXES = ("pool", "tensor")
MIB = 1 << 20
CHUNK = 64
GROUP = 4


def ring_order(size):
    return list(range(0, size, 2)) + list(range(size - 1, 0, -2))


def ring_pairs(size):
    ring = ring_order(size)
    return [
        (p * size + ring[k], p * size + ring[(k + 1 - 2 * p) % size])
        for p in range(2)
        for k in range(size)
    ]


def sibling_pairs(size):
    return [(p * size + t, (1 - p) * size + t) for p in range(2) for t in range(size)]


def fetch_kernel(count, *refs):
    sems = refs[2 * count]
    copies = [
        pltpu.make_async_copy(refs[i], refs[count + i], sems.at[i]) for i in range(count)
    ]
    for copy in copies:
        copy.start()
    for copy in copies:
        copy.wait()


def fetch(*arrays):
    count = len(arrays)
    size = sum(x.size * x.dtype.itemsize for x in arrays)
    return pl.pallas_call(
        lambda *refs: fetch_kernel(count, *refs),
        in_specs=[pl.BlockSpec(memory_space=pl.ANY)] * count,
        out_specs=[pl.BlockSpec(memory_space=pltpu.VMEM)] * count,
        out_shape=[pltpu.VMEM(x.shape, x.dtype) for x in arrays],
        scratch_shapes=[pltpu.SemaphoreType.DMA((count,))],
        compiler_params=pltpu.CompilerParams(vmem_limit_bytes=MIB),
        cost_estimate=pl.CostEstimate(flops=0, bytes_accessed=2 * size, transcendentals=0),
    )(*[pltpu.with_memory_space_constraint(x, pltpu.HBM) for x in arrays])


def project_kernel(count, depth, *refs):
    blocks = refs[:count]
    slots_ref, wq_ref, wkv_ref, out_ref, acc = refs[count:]
    query_cols = wq_ref.shape[1]
    for start in range(0, wq_ref.shape[0], depth):
        cut = slice(start, start + depth)
        part = jnp.concatenate([b[:, cut] for b in blocks], axis=0)
        query = jnp.dot(part, wq_ref[cut, :], preferred_element_type=jnp.float32)
        keyval = jnp.dot(part, wkv_ref[cut, :], preferred_element_type=jnp.float32)
        if start == 0:
            acc[:, :query_cols] = query
            acc[:, query_cols:] = keyval
        else:
            acc[:, :query_cols] += query
            acc[:, query_cols:] += keyval
    requests = acc.shape[0]
    ids = lax.broadcasted_iota(jnp.int32, (requests, requests), 0)
    order = (slots_ref[...] == ids).astype(jnp.bfloat16)
    out_ref[...] = jnp.dot(
        order, acc[...].astype(jnp.bfloat16), preferred_element_type=jnp.float32
    ).astype(jnp.bfloat16)


def project(blocks, slots_local, w_query, w_keyval, depth):
    count = len(blocks)
    requests = blocks[0].shape[0] * count
    width = w_query.shape[1] + w_keyval.shape[1]
    whole = pl.BlockSpec(memory_space=pltpu.VMEM)
    return pl.pallas_call(
        lambda *refs: project_kernel(count, depth, *refs),
        in_specs=[whole] * (count + 3),
        out_specs=whole,
        out_shape=jax.ShapeDtypeStruct((requests, width), jnp.bfloat16),
        scratch_shapes=[pltpu.VMEM((requests, width), jnp.float32)],
        compiler_params=pltpu.CompilerParams(vmem_limit_bytes=16 * MIB),
        name="project",
    )(
        *blocks,
        slots_local,
        pltpu.with_memory_space_constraint(w_query, pltpu.VMEM),
        pltpu.with_memory_space_constraint(w_keyval, pltpu.VMEM),
    )


def attend_kernel(query_cols, len_ref, arrived_ref, keys_hbm, values_hbm, out_ref,
                  keys_ref, values_ref, full, scores, probs, weights, packed, sems):
    slots, cached, kv_width = keys_ref.shape
    chunk = min(cached, CHUNK)
    chunks = cached // chunk

    def copy(which, s, c):
        src, dst = ((keys_hbm, keys_ref), (values_hbm, values_ref))[which]
        cut = pl.ds(c * chunk, chunk)
        return pltpu.make_async_copy(src.at[s, cut], dst.at[s, cut], sems.at[which, s, c])

    def each(which, s, act):
        for c in range(chunks):
            if c == 0:
                act(copy(which, s, c))
            else:
                pl.when(len_ref[s] > c * chunk)(lambda c=c: act(copy(which, s, c)))

    for which in range(2):
        for s in range(slots):
            each(which, s, lambda x: x.start())
    for s in range(slots):
        for c in range(1, chunks):

            @pl.when(len_ref[s] <= c * chunk)
            def _(s=s, c=c):
                values_ref[s, c * chunk : (c + 1) * chunk, :] = jnp.zeros(
                    (chunk, kv_width), values_ref.dtype
                )

    rows = arrived_ref.shape[0]
    devices = rows // slots
    per_dev = query_cols // HD
    kv_cols = arrived_ref.shape[1] - query_cols
    pieces = HD // kv_cols
    group = HEADS // KVH
    scale = HD ** (-0.5)
    for i in range(per_dev):
        full[i] = arrived_ref[:, i * HD : (i + 1) * HD].astype(jnp.float32)
    target = lax.broadcasted_iota(jnp.int32, (rows, rows), 0)
    source = lax.broadcasted_iota(jnp.int32, (rows, rows), 1)
    holder = ((target // slots) * per_dev // group) * pieces
    fresh = arrived_ref[:, query_cols:]
    for which in range(2):
        for i in range(pieces):
            wanted = (which * (devices // 2) + holder + i) * slots + target % slots
            pick = (source == wanted).astype(jnp.bfloat16)
            full[per_dev + which, :, i * kv_cols : (i + 1) * kv_cols] = jnp.dot(
                pick, fresh, preferred_element_type=jnp.float32
            )
    row = lax.broadcasted_iota(jnp.int32, (HEADS, 1), 0)
    kv_head = ((row % devices) * per_dev + row // devices) // group
    lane_head = lax.broadcasted_iota(jnp.int32, (HEADS, kv_width), 1) // HD
    block_mask = lane_head == kv_head
    position = lax.broadcasted_iota(jnp.int32, (HEADS, cached), 1)

    def of_slot(s, i):
        return full[i, pl.ds(s, devices, stride=slots), :]

    def repeated(s, i):
        return jnp.concatenate([of_slot(s, i)] * per_dev, axis=0)

    owns = []
    for s in range(slots):
        if s % GROUP == 0:
            for other in range(s, min(s + GROUP, slots)):
                each(0, other, lambda x: x.wait())
        q = jnp.concatenate([of_slot(s, i) for i in range(per_dev)], axis=0)
        wide = jnp.where(block_mask, jnp.concatenate([q] * KVH, axis=1), 0.0).astype(jnp.bfloat16)
        scores[s] = lax.dot_general(
            wide, keys_ref[s], (((1,), (1,)), ((), ())), preferred_element_type=jnp.float32
        )
        owns.append(jnp.sum(q * repeated(s, per_dev), axis=1, keepdims=True) * scale)
    for s in range(slots):
        sc = jnp.where(position < len_ref[s], scores[s] * scale, -1e30)
        top = jnp.maximum(jnp.max(sc, axis=1, keepdims=True), owns[s])
        pr = jnp.exp(sc - top)
        own_prob = jnp.exp(owns[s] - top)
        total = jnp.sum(pr, axis=1, keepdims=True) + own_prob
        probs[s] = pr.astype(jnp.bfloat16)
        own_low = own_prob.astype(jnp.bfloat16).astype(jnp.float32)
        weights[s] = jnp.concatenate([own_low, total], axis=1)
    for s in range(slots):
        if s % GROUP == 0:
            for other in range(s, min(s + GROUP, slots)):
                each(1, other, lambda x: x.wait())
        all_heads = jnp.dot(probs[s], values_ref[s], preferred_element_type=jnp.float32)
        mine = jnp.zeros((HEADS, HD), jnp.float32)
        for k in range(KVH):
            mine = jnp.where(kv_head == k, all_heads[:, k * HD : (k + 1) * HD], mine)
        wt = weights[s]
        mine = (mine + wt[:, 0:1] * repeated(s, per_dev + 1)) / wt[:, 1:2]
        for i in range(per_dev):
            packed[i, pl.ds(s, devices, stride=slots), :] = mine[i * devices : (i + 1) * devices]
    for i in range(per_dev):
        out_ref[:, i * HD : (i + 1) * HD] = packed[i].astype(jnp.bfloat16)


def attend(slot_len, arrived, key_cache, value_cache, query_cols):
    slots, cached, _ = key_cache.shape
    rows = arrived.shape[0]
    whole = pl.BlockSpec(memory_space=pltpu.VMEM)
    return pl.pallas_call(
        lambda *refs: attend_kernel(query_cols, *refs),
        in_specs=[pl.BlockSpec(memory_space=pltpu.SMEM), whole]
        + [pl.BlockSpec(memory_space=pl.ANY)] * 2,
        out_specs=whole,
        out_shape=jax.ShapeDtypeStruct((rows, query_cols), jnp.bfloat16),
        scratch_shapes=[
            pltpu.VMEM(key_cache.shape, key_cache.dtype),
            pltpu.VMEM(value_cache.shape, value_cache.dtype),
            pltpu.VMEM((query_cols // HD + 2, rows, HD), jnp.float32),
            pltpu.VMEM((slots, HEADS, cached), jnp.float32),
            pltpu.VMEM((slots, HEADS, cached), jnp.bfloat16),
            pltpu.VMEM((slots, HEADS, 2), jnp.float32),
            pltpu.VMEM((query_cols // HD, rows, HD), jnp.float32),
            pltpu.SemaphoreType.DMA((2, slots, -(-cached // CHUNK))),
        ],
        compiler_params=pltpu.CompilerParams(vmem_limit_bytes=32 * MIB),
        name="attend",
    )(
        slot_len,
        arrived,
        pltpu.with_memory_space_constraint(key_cache, pltpu.HBM),
        pltpu.with_memory_space_constraint(value_cache, pltpu.HBM),
    )


def output_kernel(cuts, cols, fetching, slots_ref, back_ref, w_ref, *outs):
    requests = back_ref.shape[0]
    ids = lax.broadcasted_iota(jnp.int32, (requests, slots_ref.shape[1]), 0)
    order = (slots_ref[...] == ids).astype(jnp.bfloat16)
    starts = range(0, w_ref.shape[1], cols)
    copies = []
    if fetching:
        held, sems = outs[len(cuts)], outs[len(cuts) + 1]
        for i, start in enumerate(starts):
            cut = pl.ds(start, cols)
            copies.append(pltpu.make_async_copy(w_ref.at[:, cut], held.at[:, cut], sems.at[i]))
            copies[-1].start()
        w_ref = held
    rows = lax.dot_general(
        order, back_ref[...], (((0,), (0,)), ((), ())), preferred_element_type=jnp.float32
    ).astype(jnp.bfloat16)
    for i, start in enumerate(starts):
        cut = slice(start, start + cols)
        if fetching:
            copies[i].wait()
        out = jnp.dot(rows, w_ref[:, cut], preferred_element_type=jnp.float32).astype(jnp.bfloat16)
        first = 0
        for size, ref in zip(cuts, outs[: len(cuts)], strict=True):
            ref[:, cut] = out[first : first + size]
            first += size


def output(cuts, slots_local, returned, w_out, cols, fetching):
    model = w_out.shape[1]
    whole = pl.BlockSpec(memory_space=pltpu.VMEM)
    out_shape = [jax.ShapeDtypeStruct((size, model), jnp.bfloat16) for size in cuts]
    if fetching:
        out_shape.append(pltpu.VMEM(w_out.shape, w_out.dtype))
    place = pltpu.HBM if fetching else pltpu.VMEM
    return pl.pallas_call(
        lambda *refs: output_kernel(cuts, cols, fetching, *refs),
        in_specs=[whole] * 2 + [pl.BlockSpec(memory_space=pl.ANY) if fetching else whole],
        out_specs=[whole] * len(out_shape),
        out_shape=out_shape,
        scratch_shapes=[pltpu.SemaphoreType.DMA((model // cols,))] if fetching else [],
        compiler_params=pltpu.CompilerParams(vmem_limit_bytes=12 * MIB),
    )(slots_local, returned, pltpu.with_memory_space_constraint(w_out, place))


def add_up_kernel(starts, extra, block, *refs):
    outs = refs[2 * len(starts) + extra :]
    arrivals = refs[2 * len(starts) : 2 * len(starts) + extra]
    for i, (start, out) in enumerate(zip(starts, outs, strict=True)):
        cut = slice(start, start + block)
        total = refs[2 * i][cut, :].astype(jnp.float32) + refs[2 * i + 1][cut, :].astype(jnp.float32)
        for arrived in arrivals:
            total += arrived[...].astype(jnp.float32)
        out[...] = total.astype(jnp.bfloat16)


def add_up(pieces, arrivals, block):
    operands = [x for own, got, _ in pieces for x in (own, got)] + list(arrivals)
    starts = [start for _, _, start in pieces]
    model = operands[0].shape[1]
    whole = pl.BlockSpec(memory_space=pltpu.VMEM)
    return pl.pallas_call(
        lambda *refs: add_up_kernel(starts, len(arrivals), block, *refs),
        in_specs=[whole] * len(operands),
        out_specs=[whole] * len(starts),
        out_shape=[jax.ShapeDtypeStruct((block, model), jnp.bfloat16)] * len(starts),
        compiler_params=pltpu.CompilerParams(vmem_limit_bytes=8 * MIB),
    )(*operands)


def body(rows, norm_gain, w_query, w_keyval, w_out, key_cache, value_cache, lengths, slot_of):
    size = lax.axis_size("tensor")
    devices = lax.axis_size(AXES)
    half = size // 2
    block = rows.shape[0]
    slots_dev = key_cache.shape[0]
    query_cols = w_query.shape[1]
    forward = lambda x: lax.ppermute(x, AXES, ring_pairs(size))
    swap = lambda x: lax.ppermute(x, AXES, sibling_pairs(size))

    pool = lax.axis_index("pool")
    tensor = lax.axis_index("tensor")
    way = 1 - 2 * pool
    place = jnp.where(tensor % 2 == 0, tensor // 2, size - 1 - tensor // 2)

    def device_at(steps, owner):
        at = (place + way * steps + 2 * size) % size
        return owner * size + jnp.where(at < half, 2 * at, 2 * (size - 1 - at) + 1)

    slot_blocks = slot_of.reshape(devices, block)

    def slots_in(order):
        pick = jnp.stack(order)[:, None] == jnp.arange(devices, dtype=jnp.int32)[None, :]
        return jnp.sum(jnp.where(pick[:, :, None], slot_blocks[None], 0), axis=1).reshape(-1)

    values32 = rows.astype(jnp.float32)
    normed = (
        values32 * lax.rsqrt(jnp.mean(values32 * values32, axis=1, keepdims=True) + EPS) * norm_gain
    ).astype(jnp.bfloat16)
    a, b = normed, swap(normed)
    blocks, order = [a, b], [device_at(0, pool), device_at(0, 1 - pool)]
    for k in range(1, half):
        a, b = forward(a), forward(b)
        blocks += [a, b, swap(a), swap(b)]
        order += [
            device_at(-k, pool),
            device_at(-k, 1 - pool),
            device_at(k, 1 - pool),
            device_at(k, pool),
        ]
    a = forward(a)
    blocks += [a, swap(a)]
    order += [device_at(-half, pool), device_at(half, 1 - pool)]

    own_slots = lax.axis_index(AXES) * slots_dev + jnp.arange(slots_dev, dtype=jnp.int32)
    slot_len = jnp.sum(
        jnp.where(slot_of[None, :] == own_slots[:, None], lengths[None, :], 0), axis=1
    )
    theirs, mine = [device_at(-half, 1 - pool)], [device_at(half, pool)]
    for k in range(half - 1, 0, -1):
        theirs += [device_at(-k, 1 - pool), device_at(-k, pool)]
        mine += [device_at(k, pool), device_at(k, 1 - pool)]
    theirs += [device_at(0, 1 - pool)]
    mine += [device_at(0, pool)]
    w_query, w_keyval, slot_len, slots_local, slots_theirs, slots_mine = lax.optimization_barrier(
        (
            w_query,
            w_keyval,
            slot_len,
            slots_in(order).reshape(1, -1),
            slots_in(theirs).reshape(1, -1),
            slots_in(mine).reshape(1, -1),
        )
    )
    wq, wkv = fetch(w_query, w_keyval)
    sending = project(blocks, slots_local, wq, wkv, w_query.shape[0] // 8)
    arrived = lax.all_to_all(sending, AXES, split_axis=0, concat_axis=0, tiled=True)

    attended = attend(slot_len, arrived, key_cache, value_cache, query_cols)
    returned = lax.all_to_all(attended, AXES, split_axis=0, concat_axis=0, tiled=True)
    early = 3 * block
    rest = block * len(mine) - early
    cols = w_out.shape[1] // 8
    first, later, held = output((early, rest), slots_theirs, returned, w_out, cols, True)
    first, later = swap(first), swap(later)
    own_first, own_later = output((early, rest), slots_mine, returned, held, cols, False)

    def chip_sum(items, arrivals=()):
        pieces = [(own_first, first, i) if i < 3 else (own_later, later, i - 3) for i in items]
        return add_up([(o, g, at * block) for o, g, at in pieces], arrivals, block)

    a, b = chip_sum((0, 2))
    a = forward(a)
    b = forward(b)
    at = 1
    for k in range(half - 1, 0, -1):
        (a,) = chip_sum((at,), (a,))
        a = forward(a)
        if k > 1:
            (b,) = chip_sum((at + 3,), (b,))
            b = forward(b)
        at += 2
    across = swap(b)
    (out,) = chip_sum((at,), (a, across))
    return out


def solution(mesh):
    placed = (
        P(("groups", "pool", "tensor"), None),
        P(),
        P(None, ("pool", "tensor")),
        P(None, ("pool", "tensor")),
        P(("pool", "tensor"), None),
        P(("groups", "pool", "tensor"), None, None),
        P(("groups", "pool", "tensor"), None, None),
        P("groups"),
        P("groups"),
    )

    return jax.shard_map(
        body,
        mesh=mesh,
        in_specs=placed,
        out_specs=P(("groups", "pool", "tensor"), None),
        check_vma=False,
    )
```

```python
import jax
import jax.numpy as jnp
from jax import lax
from jax.experimental import pallas as pl
from jax.experimental.pallas import tpu as pltpu
from jax.sharding import PartitionSpec as P


HEADS = 64
KVH = 8
HD = 128
EPS = 1e-05
AXES = ("pool", "tensor")
MIB = 1 << 20
CHUNK = 64
GROUP = 4


def ring_order(size):
    return list(range(0, size, 2)) + list(range(size - 1, 0, -2))


def ring_pairs(size):
    ring = ring_order(size)
    return [
        (p * size + ring[k], p * size + ring[(k + 1 - 2 * p) % size])
        for p in range(2)
        for k in range(size)
    ]


def sibling_pairs(size):
    return [(p * size + t, (1 - p) * size + t) for p in range(2) for t in range(size)]


def norm_kernel(rows_ref, gain_ref, out_ref):
    x = rows_ref[...].astype(jnp.float32)
    mean = jnp.mean(x * x, axis=1, keepdims=True)
    out_ref[...] = (x * lax.rsqrt(mean + EPS) * gain_ref[...]).astype(jnp.bfloat16)


def norm(rows, gain):
    whole = pl.BlockSpec(memory_space=pltpu.VMEM)
    return pl.pallas_call(
        norm_kernel,
        in_specs=[whole] * 2,
        out_specs=whole,
        out_shape=jax.ShapeDtypeStruct(rows.shape, jnp.bfloat16),
        compiler_params=pltpu.CompilerParams(vmem_limit_bytes=8 * MIB),
        name="norm",
    )(*[pltpu.with_memory_space_constraint(x, pltpu.HBM) for x in (rows, gain.reshape(1, -1))])


def project_kernel(count, last, depth, *refs):
    blocks = refs[:count]
    wq_ref, wkv_ref = refs[count : count + 2]
    starts = range(0, wq_ref.shape[0], depth)
    if last:
        slots_ref, before_ref, out_ref, acc = refs[count + 2 :]
    else:
        out_ref, wq_held, wkv_held, acc, sems = refs[count + 2 :]
        copies = []
        for i, start in enumerate(starts):
            cut = pl.ds(start, depth)
            copies.append(
                [
                    pltpu.make_async_copy(wq_ref.at[cut], wq_held.at[cut], sems.at[0, i]),
                    pltpu.make_async_copy(wkv_ref.at[cut], wkv_held.at[cut], sems.at[1, i]),
                ]
            )
            for copy in copies[-1]:
                copy.start()
        wq_ref, wkv_ref = wq_held, wkv_held
    query_cols = wq_ref.shape[1]
    for i, start in enumerate(starts):
        cut = slice(start, start + depth)
        part = jnp.concatenate([b[:, cut] for b in blocks], axis=0)
        if not last:
            for copy in copies[i]:
                copy.wait()
        query = jnp.dot(part, wq_ref[cut, :], preferred_element_type=jnp.float32)
        keyval = jnp.dot(part, wkv_ref[cut, :], preferred_element_type=jnp.float32)
        if i == 0:
            acc[:, :query_cols] = query
            acc[:, query_cols:] = keyval
        else:
            acc[:, :query_cols] += query
            acc[:, query_cols:] += keyval
    if not last:
        out_ref[...] = acc[...].astype(jnp.bfloat16)
        return
    requests = slots_ref.shape[1]
    ids = lax.broadcasted_iota(jnp.int32, (requests, requests), 0)
    order = (slots_ref[...] == ids).astype(jnp.bfloat16)
    both = jnp.concatenate([before_ref[...], acc[...].astype(jnp.bfloat16)], axis=0)
    out_ref[...] = jnp.dot(order, both, preferred_element_type=jnp.float32).astype(jnp.bfloat16)


def project(blocks, weights, depth, slots=None, before=None):
    count = len(blocks)
    rows = sum(b.shape[0] for b in blocks)
    width = sum(w.shape[1] for w in weights)
    last = slots is not None
    whole = pl.BlockSpec(memory_space=pltpu.VMEM)
    place = pltpu.VMEM if last else pltpu.HBM
    operands = list(blocks) + [pltpu.with_memory_space_constraint(w, place) for w in weights]
    specs = [whole] * count + [whole if last else pl.BlockSpec(memory_space=pl.ANY)] * 2
    out_shape = [jax.ShapeDtypeStruct((slots.shape[1] if last else rows, width), jnp.bfloat16)]
    scratch = [pltpu.VMEM((rows, width), jnp.float32)]
    if last:
        operands += [slots, before]
        specs += [whole] * 2
    else:
        out_shape += [pltpu.VMEM(w.shape, w.dtype) for w in weights]
        scratch.append(pltpu.SemaphoreType.DMA((2, weights[0].shape[0] // depth)))
    return pl.pallas_call(
        lambda *refs: project_kernel(count, last, depth, *refs),
        in_specs=specs,
        out_specs=[whole] * len(out_shape),
        out_shape=out_shape,
        scratch_shapes=scratch,
        compiler_params=pltpu.CompilerParams(vmem_limit_bytes=16 * MIB),
    )(*operands)


def attend_kernel(query_cols, group, order_ref, len_ref, arrived_ref, keys_hbm, values_hbm, out_ref,
                  keys_ref, values_ref, full, packed, sems):
    slots, cached, kv_width = keys_ref.shape
    rows = arrived_ref.shape[0]
    devices = rows // slots
    per_dev = query_cols // HD
    kv_cols = arrived_ref.shape[1] - query_cols
    pieces = HD // kv_cols
    share = HEADS // KVH
    scale = HD ** (-0.5)
    chunk = min(cached, CHUNK)
    widths = range(chunk, cached + 1, chunk)

    def longest(g):
        return len_ref[order_ref[g * group + group - 1]]

    def for_width(g, act):
        most = longest(g)
        for width in widths:
            pl.when((most > width - chunk) & (most <= width))(lambda width=width: act(width))

    def copies(g, i, width):
        at = g * group + i
        s = order_ref[at]
        for which, src, dst in ((0, keys_hbm, keys_ref), (1, values_hbm, values_ref)):
            cut = pl.ds(0, width)
            yield pltpu.make_async_copy(src.at[s, cut], dst.at[at, cut], sems.at[which, at])

    def begin(g, _):
        def start(width):
            for i in range(group):
                for copy in copies(g, i, width):
                    copy.start()

        for_width(g, start)
        return 0

    lax.fori_loop(0, slots // group, begin, 0)

    for i in range(per_dev):
        full[i] = arrived_ref[:, i * HD : (i + 1) * HD].astype(jnp.float32)
    target = lax.broadcasted_iota(jnp.int32, (rows, rows), 0)
    source = lax.broadcasted_iota(jnp.int32, (rows, rows), 1)
    holder = ((target // slots) * per_dev // share) * pieces
    fresh = arrived_ref[:, query_cols:]
    for which in range(2):
        for i in range(pieces):
            wanted = (which * (devices // 2) + holder + i) * slots + target % slots
            pick = (source == wanted).astype(jnp.bfloat16)
            full[per_dev + which, :, i * kv_cols : (i + 1) * kv_cols] = jnp.dot(
                pick, fresh, preferred_element_type=jnp.float32
            )
    row = lax.broadcasted_iota(jnp.int32, (HEADS, 1), 0)
    kv_head = ((row % devices) * per_dev + row // devices) // share
    lane_head = lax.broadcasted_iota(jnp.int32, (HEADS, kv_width), 1) // HD
    block_mask = lane_head == kv_head

    def of_slot(s, i):
        return full[i, pl.ds(s, devices, stride=slots), :]

    def repeated(s, i):
        return jnp.concatenate([of_slot(s, i)] * per_dev, axis=0)

    def one_group(g, _):
        def run(width):
            for i in range(group):
                for copy in copies(g, i, width):
                    copy.wait()
            ids = [order_ref[g * group + i] for i in range(group)]
            position = lax.broadcasted_iota(jnp.int32, (HEADS, width), 1)
            scores, owns = [], []
            for i, s in enumerate(ids):
                q = jnp.concatenate([of_slot(s, j) for j in range(per_dev)], axis=0)
                wide = jnp.where(block_mask, jnp.concatenate([q] * KVH, axis=1), 0.0)
                scores.append(
                    lax.dot_general(
                        wide.astype(jnp.bfloat16),
                        keys_ref[g * group + i, :width, :],
                        (((1,), (1,)), ((), ())),
                        preferred_element_type=jnp.float32,
                    )
                )
                owns.append(jnp.sum(q * repeated(s, per_dev), axis=1, keepdims=True) * scale)
            probs, weights = [], []
            for i, s in enumerate(ids):
                sc = jnp.where(position < len_ref[s], scores[i] * scale, -1e30)
                top = jnp.maximum(jnp.max(sc, axis=1, keepdims=True), owns[i])
                pr = jnp.exp(sc - top)
                own_prob = jnp.exp(owns[i] - top)
                total = jnp.sum(pr, axis=1, keepdims=True) + own_prob
                probs.append(pr.astype(jnp.bfloat16))
                weights.append((own_prob.astype(jnp.bfloat16).astype(jnp.float32), total))
            for i, s in enumerate(ids):
                all_heads = jnp.dot(
                    probs[i],
                    values_ref[g * group + i, :width, :],
                    preferred_element_type=jnp.float32,
                )
                mine = all_heads[:, :HD]
                for k in range(1, KVH):
                    mine = jnp.where(kv_head == k, all_heads[:, k * HD : (k + 1) * HD], mine)
                own_low, total = weights[i]
                mine = (mine + own_low * repeated(s, per_dev + 1)) / total
                for j in range(per_dev):
                    packed[j, pl.ds(s, devices, stride=slots), :] = mine[
                        j * devices : (j + 1) * devices
                    ]

        for_width(g, run)
        return 0

    lax.fori_loop(0, slots // group, one_group, 0)
    for i in range(per_dev):
        out_ref[:, i * HD : (i + 1) * HD] = packed[i].astype(jnp.bfloat16)


def attend(order, slot_len, arrived, key_cache, value_cache, query_cols):
    slots = key_cache.shape[0]
    rows = arrived.shape[0]
    group = max(g for g in range(1, GROUP + 1) if slots % g == 0)
    whole = pl.BlockSpec(memory_space=pltpu.VMEM)
    return pl.pallas_call(
        lambda *refs: attend_kernel(query_cols, group, *refs),
        in_specs=[pl.BlockSpec(memory_space=pltpu.SMEM)] * 2
        + [whole]
        + [pl.BlockSpec(memory_space=pl.ANY)] * 2,
        out_specs=whole,
        out_shape=jax.ShapeDtypeStruct((rows, query_cols), jnp.bfloat16),
        scratch_shapes=[
            pltpu.VMEM(key_cache.shape, key_cache.dtype),
            pltpu.VMEM(value_cache.shape, value_cache.dtype),
            pltpu.VMEM((query_cols // HD + 2, rows, HD), jnp.float32),
            pltpu.VMEM((query_cols // HD, rows, HD), jnp.float32),
            pltpu.SemaphoreType.DMA((2, slots)),
        ],
        compiler_params=pltpu.CompilerParams(vmem_limit_bytes=32 * MIB),
        name="attend",
    )(
        order,
        slot_len,
        arrived,
        pltpu.with_memory_space_constraint(key_cache, pltpu.HBM),
        pltpu.with_memory_space_constraint(value_cache, pltpu.HBM),
    )


def output_kernel(cuts, cols, fetching, slots_ref, back_ref, w_ref, *outs):
    requests = back_ref.shape[0]
    ids = lax.broadcasted_iota(jnp.int32, (requests, slots_ref.shape[1]), 0)
    order = (slots_ref[...] == ids).astype(jnp.bfloat16)
    starts = range(0, w_ref.shape[1], cols)
    copies = []
    if fetching:
        held, sems = outs[len(cuts)], outs[len(cuts) + 1]
        for i, start in enumerate(starts):
            cut = pl.ds(start, cols)
            copies.append(pltpu.make_async_copy(w_ref.at[:, cut], held.at[:, cut], sems.at[i]))
            copies[-1].start()
        w_ref = held
    rows = lax.dot_general(
        order, back_ref[...], (((0,), (0,)), ((), ())), preferred_element_type=jnp.float32
    ).astype(jnp.bfloat16)
    for i, start in enumerate(starts):
        cut = slice(start, start + cols)
        if fetching:
            copies[i].wait()
        out = jnp.dot(rows, w_ref[:, cut], preferred_element_type=jnp.float32).astype(jnp.bfloat16)
        first = 0
        for size, ref in zip(cuts, outs[: len(cuts)], strict=True):
            ref[:, cut] = out[first : first + size]
            first += size


def output(cuts, slots_local, returned, w_out, cols, fetching):
    model = w_out.shape[1]
    whole = pl.BlockSpec(memory_space=pltpu.VMEM)
    out_shape = [jax.ShapeDtypeStruct((size, model), jnp.bfloat16) for size in cuts]
    if fetching:
        out_shape.append(pltpu.VMEM(w_out.shape, w_out.dtype))
    place = pltpu.HBM if fetching else pltpu.VMEM
    return pl.pallas_call(
        lambda *refs: output_kernel(cuts, cols, fetching, *refs),
        in_specs=[whole] * 2 + [pl.BlockSpec(memory_space=pl.ANY) if fetching else whole],
        out_specs=[whole] * len(out_shape),
        out_shape=out_shape,
        scratch_shapes=[pltpu.SemaphoreType.DMA((model // cols,))] if fetching else [],
        compiler_params=pltpu.CompilerParams(vmem_limit_bytes=12 * MIB),
    )(slots_local, returned, pltpu.with_memory_space_constraint(w_out, place))


def add_up_kernel(starts, extra, block, *refs):
    outs = refs[2 * len(starts) + extra :]
    arrivals = refs[2 * len(starts) : 2 * len(starts) + extra]
    for i, (start, out) in enumerate(zip(starts, outs, strict=True)):
        cut = slice(start, start + block)
        total = refs[2 * i][cut, :].astype(jnp.float32) + refs[2 * i + 1][cut, :].astype(jnp.float32)
        for arrived in arrivals:
            total += arrived[...].astype(jnp.float32)
        out[...] = total.astype(jnp.bfloat16)


def add_up(pieces, arrivals, block):
    operands = [x for own, got, _ in pieces for x in (own, got)] + list(arrivals)
    starts = [start for _, _, start in pieces]
    model = operands[0].shape[1]
    whole = pl.BlockSpec(memory_space=pltpu.VMEM)
    return pl.pallas_call(
        lambda *refs: add_up_kernel(starts, len(arrivals), block, *refs),
        in_specs=[whole] * len(operands),
        out_specs=[whole] * len(starts),
        out_shape=[jax.ShapeDtypeStruct((block, model), jnp.bfloat16)] * len(starts),
        compiler_params=pltpu.CompilerParams(vmem_limit_bytes=8 * MIB),
    )(*operands)


def body(rows, norm_gain, w_query, w_keyval, w_out, key_cache, value_cache, lengths, slot_of):
    size = lax.axis_size("tensor")
    devices = lax.axis_size(AXES)
    half = size // 2
    block = rows.shape[0]
    slots_dev = key_cache.shape[0]
    query_cols = w_query.shape[1]
    forward = lambda x: lax.ppermute(x, AXES, ring_pairs(size))
    swap = lambda x: lax.ppermute(x, AXES, sibling_pairs(size))

    pool = lax.axis_index("pool")
    tensor = lax.axis_index("tensor")
    way = 1 - 2 * pool
    place = jnp.where(tensor % 2 == 0, tensor // 2, size - 1 - tensor // 2)

    def device_at(steps, owner):
        at = (place + way * steps + 2 * size) % size
        return owner * size + jnp.where(at < half, 2 * at, 2 * (size - 1 - at) + 1)

    slot_blocks = slot_of.reshape(devices, block)

    def slots_in(order):
        pick = jnp.stack(order)[:, None] == jnp.arange(devices, dtype=jnp.int32)[None, :]
        return jnp.sum(jnp.where(pick[:, :, None], slot_blocks[None], 0), axis=1).reshape(-1)

    normed = norm(rows, norm_gain)
    a, b = normed, swap(normed)
    blocks, order = [a, b], [device_at(0, pool), device_at(0, 1 - pool)]
    late, late_order = [], []
    for k in range(1, half):
        a, b = forward(a), forward(b)
        blocks += [a, swap(a)]
        order += [device_at(-k, pool), device_at(k, 1 - pool)]
        into, into_order = (blocks, order) if k < half - 1 else (late, late_order)
        into += [b, swap(b)]
        into_order += [device_at(-k, 1 - pool), device_at(k, pool)]
    a = forward(a)
    late += [a, swap(a)]
    late_order += [device_at(-half, pool), device_at(half, 1 - pool)]

    own_slots = lax.axis_index(AXES) * slots_dev + jnp.arange(slots_dev, dtype=jnp.int32)
    slot_len = jnp.sum(
        jnp.where(slot_of[None, :] == own_slots[:, None], lengths[None, :], 0), axis=1
    )
    theirs, mine = [device_at(-half, 1 - pool)], [device_at(half, pool)]
    for k in range(half - 1, 0, -1):
        theirs += [device_at(-k, 1 - pool), device_at(-k, pool)]
        mine += [device_at(k, pool), device_at(k, 1 - pool)]
    theirs += [device_at(0, 1 - pool)]
    mine += [device_at(0, pool)]
    each = jnp.arange(slots_dev, dtype=jnp.int32)
    shorter = (slot_len[None, :] < slot_len[:, None]) | (
        (slot_len[None, :] == slot_len[:, None]) & (each[None, :] < each[:, None])
    )
    rank = jnp.sum(shorter.astype(jnp.int32), axis=1)
    by_length = jnp.sum(jnp.where(rank[None, :] == each[:, None], each[None, :], 0), axis=1)
    w_query, w_keyval, slot_len, by_length, slots_local, slots_early, slots_rest = (
        lax.optimization_barrier(
            (
                w_query,
                w_keyval,
                slot_len,
                by_length,
                slots_in(order + late_order).reshape(1, -1),
                slots_in(theirs + mine[:3]).reshape(1, -1),
                slots_in(mine[3:]).reshape(1, -1),
            )
        )
    )
    depth = w_query.shape[0] // 8
    early_rows, *weights = project(blocks, (w_query, w_keyval), depth)
    (sending,) = project(late, weights, depth, slots_local, early_rows)
    arrived = lax.all_to_all(sending, AXES, split_axis=0, concat_axis=0, tiled=True)

    attended = attend(by_length, slot_len, arrived, key_cache, value_cache, query_cols)
    returned = lax.all_to_all(attended, AXES, split_axis=0, concat_axis=0, tiled=True)
    early = 3 * block
    rest = block * len(mine) - early
    cols = w_out.shape[1] // 8
    first, later, own_first, held = output(
        (early, rest, early), slots_early, returned, w_out, cols, True
    )
    first, later = swap(first), swap(later)
    (own_later,) = output((rest,), slots_rest, returned, held, cols, False)

    def chip_sum(items, arrivals=()):
        pieces = [(own_first, first, i) if i < 3 else (own_later, later, i - 3) for i in items]
        return add_up([(o, g, at * block) for o, g, at in pieces], arrivals, block)

    a, b = chip_sum((0, 2))
    a = forward(a)
    b = forward(b)
    at = 1
    for k in range(half - 1, 0, -1):
        (a,) = chip_sum((at,), (a,))
        a = forward(a)
        if k > 1:
            (b,) = chip_sum((at + 3,), (b,))
            b = forward(b)
        at += 2
    across = swap(b)
    (out,) = chip_sum((at,), (a, across))
    return out


def solution(mesh):
    placed = (
        P(("groups", "pool", "tensor"), None),
        P(),
        P(None, ("pool", "tensor")),
        P(None, ("pool", "tensor")),
        P(("pool", "tensor"), None),
        P(("groups", "pool", "tensor"), None, None),
        P(("groups", "pool", "tensor"), None, None),
        P("groups"),
        P("groups"),
    )

    return jax.shard_map(
        body,
        mesh=mesh,
        in_specs=placed,
        out_specs=P(("groups", "pool", "tensor"), None),
        check_vma=False,
    )
```

```python
import jax
import jax.numpy as jnp
from jax import lax
from jax.experimental import pallas as pl
from jax.experimental.pallas import tpu as pltpu
from jax.sharding import PartitionSpec as P


HEADS = 64
KVH = 8
HD = 128
EPS = 1e-05
AXES = ("pool", "tensor")
MIB = 1 << 20
CHUNK = 64
GROUP = 4
AHEAD = 3


def ring_order(size):
    return list(range(0, size, 2)) + list(range(size - 1, 0, -2))


def ring_pairs(size):
    ring = ring_order(size)
    return [
        (p * size + ring[k], p * size + ring[(k + 1 - 2 * p) % size])
        for p in range(2)
        for k in range(size)
    ]


def sibling_pairs(size):
    return [(p * size + t, (1 - p) * size + t) for p in range(2) for t in range(size)]


def norm_kernel(rows_ref, gain_ref, out_ref):
    x = rows_ref[...].astype(jnp.float32)
    mean = jnp.mean(x * x, axis=1, keepdims=True)
    out_ref[...] = (x * lax.rsqrt(mean + EPS) * gain_ref[...]).astype(jnp.bfloat16)


def norm(rows, gain):
    whole = pl.BlockSpec(memory_space=pltpu.VMEM)
    return pl.pallas_call(
        norm_kernel,
        in_specs=[whole] * 2,
        out_specs=whole,
        out_shape=jax.ShapeDtypeStruct(rows.shape, jnp.bfloat16),
        compiler_params=pltpu.CompilerParams(vmem_limit_bytes=8 * MIB),
        name="norm",
    )(*[pltpu.with_memory_space_constraint(x, pltpu.HBM) for x in (rows, gain.reshape(1, -1))])


def project_kernel(count, last, depth, *refs):
    blocks = refs[:count]
    wq_ref, wkv_ref = refs[count : count + 2]
    starts = range(0, wq_ref.shape[0], depth)
    if last:
        slots_ref, devices_ref, before_ref, out_ref, acc, in_order = refs[count + 2 :]
    else:
        out_ref, wq_held, wkv_held, acc, sems = refs[count + 2 :]
        copies = []
        for i, start in enumerate(starts):
            cut = pl.ds(start, depth)
            copies.append(
                [
                    pltpu.make_async_copy(wq_ref.at[cut], wq_held.at[cut], sems.at[0, i]),
                    pltpu.make_async_copy(wkv_ref.at[cut], wkv_held.at[cut], sems.at[1, i]),
                ]
            )
        for some in copies[:AHEAD]:
            for copy in some:
                copy.start()
        wq_ref, wkv_ref = wq_held, wkv_held
    query_cols = wq_ref.shape[1]
    for i, start in enumerate(starts):
        cut = slice(start, start + depth)
        part = jnp.concatenate([b[:, cut] for b in blocks], axis=0)
        if not last:
            for copy in copies[i]:
                copy.wait()
            for some in copies[i + AHEAD : i + AHEAD + 1]:
                for copy in some:
                    copy.start()
        query = jnp.dot(part, wq_ref[cut, :], preferred_element_type=jnp.float32)
        keyval = jnp.dot(part, wkv_ref[cut, :], preferred_element_type=jnp.float32)
        if i == 0:
            acc[:, :query_cols] = query
            acc[:, query_cols:] = keyval
        else:
            acc[:, :query_cols] += query
            acc[:, query_cols:] += keyval
    if not last:
        out_ref[...] = acc[...].astype(jnp.bfloat16)
        return
    requests = slots_ref.shape[1]
    block = blocks[0].shape[0]
    early = before_ref.shape[0] // block
    for i in range(requests // block):
        at = pl.ds(pl.multiple_of(devices_ref[i] * block, block), block)
        if i < early:
            in_order[at, :] = before_ref[i * block : (i + 1) * block, :]
        else:
            cut = slice((i - early) * block, (i - early + 1) * block)
            in_order[at, :] = acc[cut, :].astype(jnp.bfloat16)
    ids = lax.broadcasted_iota(jnp.int32, (requests, requests), 0)
    to_slots = (slots_ref[...] == ids).astype(jnp.bfloat16)
    out_ref[...] = jnp.dot(
        to_slots, in_order[...], preferred_element_type=jnp.float32
    ).astype(jnp.bfloat16)


def project(blocks, weights, depth, slots=None, devices=None, before=None):
    count = len(blocks)
    rows = sum(b.shape[0] for b in blocks)
    width = sum(w.shape[1] for w in weights)
    last = slots is not None
    whole = pl.BlockSpec(memory_space=pltpu.VMEM)
    place = pltpu.VMEM if last else pltpu.HBM
    operands = list(blocks) + [pltpu.with_memory_space_constraint(w, place) for w in weights]
    specs = [whole] * count + [whole if last else pl.BlockSpec(memory_space=pl.ANY)] * 2
    out_shape = [jax.ShapeDtypeStruct((slots.shape[1] if last else rows, width), jnp.bfloat16)]
    scratch = [pltpu.VMEM((rows, width), jnp.float32)]
    if last:
        operands += [slots, devices, before]
        specs += [whole, pl.BlockSpec(memory_space=pltpu.SMEM), whole]
        scratch.append(pltpu.VMEM((slots.shape[1], width), jnp.bfloat16))
    else:
        out_shape += [pltpu.VMEM(w.shape, w.dtype) for w in weights]
        scratch.append(pltpu.SemaphoreType.DMA((2, weights[0].shape[0] // depth)))
    return pl.pallas_call(
        lambda *refs: project_kernel(count, last, depth, *refs),
        in_specs=specs,
        out_specs=[whole] * len(out_shape),
        out_shape=out_shape,
        scratch_shapes=scratch,
        compiler_params=pltpu.CompilerParams(vmem_limit_bytes=16 * MIB),
    )(*operands)


def attend_kernel(query_cols, group, order_ref, len_ref, arrived_ref, keys_hbm, values_hbm, out_ref,
                  keys_ref, values_ref, full, packed, sems):
    slots, cached, kv_width = keys_ref.shape
    rows = arrived_ref.shape[0]
    devices = rows // slots
    per_dev = query_cols // HD
    kv_cols = arrived_ref.shape[1] - query_cols
    pieces = HD // kv_cols
    share = HEADS // KVH
    scale = HD ** (-0.5)
    chunk = min(cached, CHUNK)
    widths = range(chunk, cached + 1, chunk)

    def longest(g):
        return len_ref[order_ref[g * group + group - 1]]

    def for_width(g, act):
        most = longest(g)
        for width in widths:
            pl.when((most > width - chunk) & (most <= width))(lambda width=width: act(width))

    def copies(g, i, width):
        at = g * group + i
        s = order_ref[at]
        for which, src, dst in ((0, keys_hbm, keys_ref), (1, values_hbm, values_ref)):
            cut = pl.ds(0, width)
            yield pltpu.make_async_copy(src.at[s, cut], dst.at[at, cut], sems.at[which, at])

    def begin(g, _):
        def start(width):
            for i in range(group):
                for copy in copies(g, i, width):
                    copy.start()

        for_width(g, start)
        return 0

    groups = slots // group
    lax.fori_loop(0, min(2, groups), begin, 0)

    for i in range(per_dev):
        full[i] = arrived_ref[:, i * HD : (i + 1) * HD].astype(jnp.float32)
    target = lax.broadcasted_iota(jnp.int32, (rows, rows), 0)
    source = lax.broadcasted_iota(jnp.int32, (rows, rows), 1)
    holder = ((target // slots) * per_dev // share) * pieces
    fresh = arrived_ref[:, query_cols:]
    for which in range(2):
        for i in range(pieces):
            wanted = (which * (devices // 2) + holder + i) * slots + target % slots
            pick = (source == wanted).astype(jnp.bfloat16)
            full[per_dev + which, :, i * kv_cols : (i + 1) * kv_cols] = jnp.dot(
                pick, fresh, preferred_element_type=jnp.float32
            )
    row = lax.broadcasted_iota(jnp.int32, (HEADS, 1), 0)
    kv_head = ((row % devices) * per_dev + row // devices) // share
    lane_head = lax.broadcasted_iota(jnp.int32, (HEADS, kv_width), 1) // HD
    block_mask = lane_head == kv_head

    def of_slot(s, i):
        return full[i, pl.ds(s, devices, stride=slots), :]

    def repeated(s, i):
        return jnp.concatenate([of_slot(s, i)] * per_dev, axis=0)

    def one_group(g, _):
        def run(width):
            for i in range(group):
                for copy in copies(g, i, width):
                    copy.wait()

            @pl.when(g + 2 < groups)
            def _():
                begin(g + 2, 0)

            ids = [order_ref[g * group + i] for i in range(group)]
            position = lax.broadcasted_iota(jnp.int32, (HEADS, width), 1)
            scores, owns = [], []
            for i, s in enumerate(ids):
                q = jnp.concatenate([of_slot(s, j) for j in range(per_dev)], axis=0)
                wide = jnp.where(block_mask, jnp.concatenate([q] * KVH, axis=1), 0.0)
                scores.append(
                    lax.dot_general(
                        wide.astype(jnp.bfloat16),
                        keys_ref[g * group + i, :width, :],
                        (((1,), (1,)), ((), ())),
                        preferred_element_type=jnp.float32,
                    )
                )
                owns.append(jnp.sum(q * repeated(s, per_dev), axis=1, keepdims=True) * scale)
            probs, weights = [], []
            for i, s in enumerate(ids):
                sc = jnp.where(position < len_ref[s], scores[i] * scale, -1e30)
                top = jnp.maximum(jnp.max(sc, axis=1, keepdims=True), owns[i])
                pr = jnp.exp(sc - top)
                own_prob = jnp.exp(owns[i] - top)
                total = jnp.sum(pr, axis=1, keepdims=True) + own_prob
                probs.append(pr.astype(jnp.bfloat16))
                weights.append((own_prob.astype(jnp.bfloat16).astype(jnp.float32), total))
            for i, s in enumerate(ids):
                all_heads = jnp.dot(
                    probs[i],
                    values_ref[g * group + i, :width, :],
                    preferred_element_type=jnp.float32,
                )
                mine = all_heads[:, :HD]
                for k in range(1, KVH):
                    mine = jnp.where(kv_head == k, all_heads[:, k * HD : (k + 1) * HD], mine)
                own_low, total = weights[i]
                mine = (mine + own_low * repeated(s, per_dev + 1)) / total
                for j in range(per_dev):
                    packed[j, pl.ds(s, devices, stride=slots), :] = mine[
                        j * devices : (j + 1) * devices
                    ]

        for_width(g, run)
        return 0

    lax.fori_loop(0, groups, one_group, 0)
    for i in range(per_dev):
        out_ref[:, i * HD : (i + 1) * HD] = packed[i].astype(jnp.bfloat16)


def attend(order, slot_len, arrived, key_cache, value_cache, query_cols):
    slots = key_cache.shape[0]
    rows = arrived.shape[0]
    group = max(g for g in range(1, GROUP + 1) if slots % g == 0)
    whole = pl.BlockSpec(memory_space=pltpu.VMEM)
    return pl.pallas_call(
        lambda *refs: attend_kernel(query_cols, group, *refs),
        in_specs=[pl.BlockSpec(memory_space=pltpu.SMEM)] * 2
        + [whole]
        + [pl.BlockSpec(memory_space=pl.ANY)] * 2,
        out_specs=whole,
        out_shape=jax.ShapeDtypeStruct((rows, query_cols), jnp.bfloat16),
        scratch_shapes=[
            pltpu.VMEM(key_cache.shape, key_cache.dtype),
            pltpu.VMEM(value_cache.shape, value_cache.dtype),
            pltpu.VMEM((query_cols // HD + 2, rows, HD), jnp.float32),
            pltpu.VMEM((query_cols // HD, rows, HD), jnp.float32),
            pltpu.SemaphoreType.DMA((2, slots)),
        ],
        compiler_params=pltpu.CompilerParams(vmem_limit_bytes=32 * MIB),
        name="attend",
    )(
        order,
        slot_len,
        arrived,
        pltpu.with_memory_space_constraint(key_cache, pltpu.HBM),
        pltpu.with_memory_space_constraint(value_cache, pltpu.HBM),
    )


def output_kernel(cuts, cols, block, first_block, fetching, slots_ref, devices_ref, back_ref, w_ref, *outs):
    requests = back_ref.shape[0]
    *outs, in_order = outs
    ids = lax.broadcasted_iota(jnp.int32, (requests, requests), 0)
    to_slots = (slots_ref[...] == ids).astype(jnp.bfloat16)
    starts = range(0, w_ref.shape[1], cols)
    copies = []
    if fetching:
        held, sems = outs[len(cuts)], outs[len(cuts) + 1]
        for i, start in enumerate(starts):
            cut = pl.ds(start, cols)
            copies.append(pltpu.make_async_copy(w_ref.at[:, cut], held.at[:, cut], sems.at[i]))
        for copy in copies[:AHEAD]:
            copy.start()
        w_ref = held
    in_order[...] = lax.dot_general(
        to_slots, back_ref[...], (((0,), (0,)), ((), ())), preferred_element_type=jnp.float32
    ).astype(jnp.bfloat16)
    rows = jnp.concatenate(
        [
            in_order[pl.ds(pl.multiple_of(devices_ref[first_block + i] * block, block), block), :]
            for i in range(sum(cuts) // block)
        ],
        axis=0,
    )
    for i, start in enumerate(starts):
        cut = slice(start, start + cols)
        if fetching:
            copies[i].wait()
            for copy in copies[i + AHEAD : i + AHEAD + 1]:
                copy.start()
        out = jnp.dot(rows, w_ref[:, cut], preferred_element_type=jnp.float32).astype(jnp.bfloat16)
        first = 0
        for size, ref in zip(cuts, outs[: len(cuts)], strict=True):
            ref[:, cut] = out[first : first + size]
            first += size


def output(cuts, block, first_block, slots, devices, returned, w_out, cols, fetching):
    model = w_out.shape[1]
    whole = pl.BlockSpec(memory_space=pltpu.VMEM)
    out_shape = [jax.ShapeDtypeStruct((size, model), jnp.bfloat16) for size in cuts]
    if fetching:
        out_shape.append(pltpu.VMEM(w_out.shape, w_out.dtype))
    place = pltpu.HBM if fetching else pltpu.VMEM
    return pl.pallas_call(
        lambda *refs: output_kernel(cuts, cols, block, first_block, fetching, *refs),
        in_specs=[whole, pl.BlockSpec(memory_space=pltpu.SMEM), whole]
        + [pl.BlockSpec(memory_space=pl.ANY) if fetching else whole],
        out_specs=[whole] * len(out_shape),
        out_shape=out_shape,
        scratch_shapes=([pltpu.SemaphoreType.DMA((model // cols,))] if fetching else [])
        + [pltpu.VMEM(returned.shape, jnp.bfloat16)],
        compiler_params=pltpu.CompilerParams(vmem_limit_bytes=12 * MIB),
    )(slots, devices, returned, pltpu.with_memory_space_constraint(w_out, place))


def add_up_kernel(starts, extra, block, *refs):
    outs = refs[2 * len(starts) + extra :]
    arrivals = refs[2 * len(starts) : 2 * len(starts) + extra]
    for i, (start, out) in enumerate(zip(starts, outs, strict=True)):
        cut = slice(start, start + block)
        total = refs[2 * i][cut, :].astype(jnp.float32) + refs[2 * i + 1][cut, :].astype(jnp.float32)
        for arrived in arrivals:
            total += arrived[...].astype(jnp.float32)
        out[...] = total.astype(jnp.bfloat16)


def add_up(pieces, arrivals, block):
    operands = [x for own, got, _ in pieces for x in (own, got)] + list(arrivals)
    starts = [start for _, _, start in pieces]
    model = operands[0].shape[1]
    whole = pl.BlockSpec(memory_space=pltpu.VMEM)
    return pl.pallas_call(
        lambda *refs: add_up_kernel(starts, len(arrivals), block, *refs),
        in_specs=[whole] * len(operands),
        out_specs=[whole] * len(starts),
        out_shape=[jax.ShapeDtypeStruct((block, model), jnp.bfloat16)] * len(starts),
        compiler_params=pltpu.CompilerParams(vmem_limit_bytes=8 * MIB),
    )(*operands)


def body(rows, norm_gain, w_query, w_keyval, w_out, key_cache, value_cache, lengths, slot_of):
    size = lax.axis_size("tensor")
    devices = lax.axis_size(AXES)
    half = size // 2
    block = rows.shape[0]
    slots_dev = key_cache.shape[0]
    query_cols = w_query.shape[1]
    forward = lambda x: lax.ppermute(x, AXES, ring_pairs(size))
    swap = lambda x: lax.ppermute(x, AXES, sibling_pairs(size))

    pool = lax.axis_index("pool")
    tensor = lax.axis_index("tensor")
    way = 1 - 2 * pool
    place = jnp.where(tensor % 2 == 0, tensor // 2, size - 1 - tensor // 2)

    def device_at(steps, owner):
        at = (place + way * steps + 2 * size) % size
        return owner * size + jnp.where(at < half, 2 * at, 2 * (size - 1 - at) + 1)

    order = [device_at(0, pool), device_at(0, 1 - pool)]
    late_order = []
    for k in range(1, half):
        order += [device_at(-k, pool), device_at(k, 1 - pool)]
        into = order if k < half - 1 else late_order
        into += [device_at(-k, 1 - pool), device_at(k, pool)]
    late_order += [device_at(-half, pool), device_at(half, 1 - pool)]
    own_slots = lax.axis_index(AXES) * slots_dev + jnp.arange(slots_dev, dtype=jnp.int32)
    slot_len = jnp.sum(
        jnp.where(slot_of[None, :] == own_slots[:, None], lengths[None, :], 0), axis=1
    )
    theirs, mine = [device_at(-half, 1 - pool)], [device_at(half, pool)]
    for k in range(half - 1, 0, -1):
        theirs += [device_at(-k, 1 - pool), device_at(-k, pool)]
        mine += [device_at(k, pool), device_at(k, 1 - pool)]
    theirs += [device_at(0, 1 - pool)]
    mine += [device_at(0, pool)]
    each = jnp.arange(slots_dev, dtype=jnp.int32)
    shorter = (slot_len[None, :] < slot_len[:, None]) | (
        (slot_len[None, :] == slot_len[:, None]) & (each[None, :] < each[:, None])
    )
    rank = jnp.sum(shorter.astype(jnp.int32), axis=1)
    by_length = jnp.sum(jnp.where(rank[None, :] == each[:, None], each[None, :], 0), axis=1)
    owners = jnp.stack(order + late_order + theirs + mine)
    index = (slot_len, by_length, owners, slot_of.reshape(1, -1))

    normed = norm(rows, norm_gain)
    a, b = normed, swap(normed)
    b, index = lax.optimization_barrier((b, index))
    slot_len, by_length, owners, slot_row = index
    blocks, late = [a, b], []
    for k in range(1, half):
        a, b = forward(a), forward(b)
        blocks += [a, swap(a)]
        into = blocks if k < half - 1 else late
        into += [b, swap(b)]
    a = forward(a)
    late += [a, swap(a)]

    depth = w_query.shape[0] // 8
    early_rows, *weights = project(blocks, (w_query, w_keyval), depth)
    (sending,) = project(late, weights, depth, slot_row, owners, early_rows)
    arrived = lax.all_to_all(sending, AXES, split_axis=0, concat_axis=0, tiled=True)

    attended = attend(by_length, slot_len, arrived, key_cache, value_cache, query_cols)
    returned = lax.all_to_all(attended, AXES, split_axis=0, concat_axis=0, tiled=True)
    early = 3 * block
    rest = block * len(mine) - early
    cols = w_out.shape[1] // 8
    first, later, own_first, held = output(
        (early, rest, early), block, devices, slot_row, owners, returned, w_out, cols, True
    )
    first, later = swap(first), swap(later)
    begun = devices + (2 * early + rest) // block
    (own_later,) = output((rest,), block, begun, slot_row, owners, returned, held, cols, False)

    def chip_sum(items, arrivals=()):
        pieces = [(own_first, first, i) if i < 3 else (own_later, later, i - 3) for i in items]
        return add_up([(o, g, at * block) for o, g, at in pieces], arrivals, block)

    a, b = chip_sum((0, 2))
    a = forward(a)
    b = forward(b)
    at = 1
    for k in range(half - 1, 0, -1):
        (a,) = chip_sum((at,), (a,))
        a = forward(a)
        if k > 1:
            (b,) = chip_sum((at + 3,), (b,))
            b = forward(b)
        at += 2
    across = swap(b)
    (out,) = chip_sum((at,), (a, across))
    return out


def solution(mesh):
    placed = (
        P(("groups", "pool", "tensor"), None),
        P(),
        P(None, ("pool", "tensor")),
        P(None, ("pool", "tensor")),
        P(("pool", "tensor"), None),
        P(("groups", "pool", "tensor"), None, None),
        P(("groups", "pool", "tensor"), None, None),
        P("groups"),
        P("groups"),
    )

    return jax.shard_map(
        body,
        mesh=mesh,
        in_specs=placed,
        out_specs=P(("groups", "pool", "tensor"), None),
        check_vma=False,
    )
```

```python
import jax
import jax.numpy as jnp
from jax import lax
from jax.experimental import pallas as pl
from jax.experimental.pallas import tpu as pltpu
from jax.sharding import PartitionSpec as P


HEADS = 64
KVH = 8
HD = 128
EPS = 1e-05
AXES = ("pool", "tensor")
MIB = 1 << 20
CHUNK = 64
GROUP = 4
PIECES = 4
DEPTH = 1024


def ring_order(size):
    return list(range(0, size, 2)) + list(range(size - 1, 0, -2))


def ring_pairs(size):
    ring = ring_order(size)
    return [
        (p * size + ring[k], p * size + ring[(k + 1 - 2 * p) % size])
        for p in range(2)
        for k in range(size)
    ]


def sibling_pairs(size):
    return [(p * size + t, (1 - p) * size + t) for p in range(2) for t in range(size)]


def norm_kernel(rows_ref, gain_ref, out_ref):
    x = rows_ref[...].astype(jnp.float32)
    mean = jnp.mean(x * x, axis=1, keepdims=True)
    out_ref[...] = (x * lax.rsqrt(mean + EPS) * gain_ref[...]).astype(jnp.bfloat16)


def norm(rows, gain):
    whole = pl.BlockSpec(memory_space=pltpu.VMEM)
    return pl.pallas_call(
        norm_kernel,
        in_specs=[whole] * 2,
        out_specs=whole,
        out_shape=jax.ShapeDtypeStruct(rows.shape, jnp.bfloat16),
        compiler_params=pltpu.CompilerParams(vmem_limit_bytes=8 * MIB),
        name="norm",
    )(*[pltpu.with_memory_space_constraint(x, pltpu.HBM) for x in (rows, gain.reshape(1, -1))])


def fetch_kernel(count, start, *refs):
    sems = refs[2 * count]
    copies = [
        pltpu.make_async_copy(
            refs[i].at[pl.ds(start, refs[count + i].shape[0])], refs[count + i], sems.at[i]
        )
        for i in range(count)
    ]
    for copy in copies:
        copy.start()
    for copy in copies:
        copy.wait()


def fetch(start, rows, *arrays):
    count = len(arrays)
    size = sum(rows * x.shape[1] * x.dtype.itemsize for x in arrays)
    return pl.pallas_call(
        lambda *refs: fetch_kernel(count, start, *refs),
        in_specs=[pl.BlockSpec(memory_space=pl.ANY)] * count,
        out_specs=[pl.BlockSpec(memory_space=pltpu.VMEM)] * count,
        out_shape=[pltpu.VMEM((rows, x.shape[1]), x.dtype) for x in arrays],
        scratch_shapes=[pltpu.SemaphoreType.DMA((count,))],
        compiler_params=pltpu.CompilerParams(vmem_limit_bytes=MIB),
        cost_estimate=pl.CostEstimate(flops=0, bytes_accessed=2 * size, transcendentals=0),
    )(*[pltpu.with_memory_space_constraint(x, pltpu.HBM) for x in arrays])


def project_kernel(count, held, last, *refs):
    blocks = refs[:count]
    pieces = [refs[count + 2 * i : count + 2 * i + 2] for i in range(held)]
    if last:
        slots_ref, before_ref, out_ref, acc = refs[count + 2 * held :]
    else:
        out_ref, acc = refs[count + 2 * held :]
    query_cols = pieces[0][0].shape[1]
    rows = pieces[0][0].shape[0]
    depth = min(rows, DEPTH)
    for i, (wq_ref, wkv_ref) in enumerate(pieces):
        for start in range(0, rows, depth):
            cut = slice(start, start + depth)
            at = i * rows + start
            part = jnp.concatenate([b[:, at : at + depth] for b in blocks], axis=0)
            query = jnp.dot(part, wq_ref[cut, :], preferred_element_type=jnp.float32)
            keyval = jnp.dot(part, wkv_ref[cut, :], preferred_element_type=jnp.float32)
            if at == 0:
                acc[:, :query_cols] = query
                acc[:, query_cols:] = keyval
            else:
                acc[:, :query_cols] += query
                acc[:, query_cols:] += keyval
    if not last:
        out_ref[...] = acc[...].astype(jnp.bfloat16)
        return
    requests = slots_ref.shape[1]
    ids = lax.broadcasted_iota(jnp.int32, (requests, requests), 0)
    order = (slots_ref[...] == ids).astype(jnp.bfloat16)
    both = jnp.concatenate([before_ref[...], acc[...].astype(jnp.bfloat16)], axis=0)
    out_ref[...] = jnp.dot(order, both, preferred_element_type=jnp.float32).astype(jnp.bfloat16)


def project(blocks, pieces, slots=None, before=None):
    count = len(blocks)
    rows = sum(b.shape[0] for b in blocks)
    width = sum(w.shape[1] for w in pieces[0])
    last = slots is not None
    whole = pl.BlockSpec(memory_space=pltpu.VMEM)
    operands = list(blocks)
    operands += [pltpu.with_memory_space_constraint(w, pltpu.VMEM) for p in pieces for w in p]
    operands += [slots, before] if last else []
    out_rows = slots.shape[1] if last else rows
    return pl.pallas_call(
        lambda *refs: project_kernel(count, len(pieces), last, *refs),
        in_specs=[whole] * len(operands),
        out_specs=whole,
        out_shape=jax.ShapeDtypeStruct((out_rows, width), jnp.bfloat16),
        scratch_shapes=[pltpu.VMEM((rows, width), jnp.float32)],
        compiler_params=pltpu.CompilerParams(vmem_limit_bytes=16 * MIB),
    )(*operands)


def attend_kernel(query_cols, group, order_ref, len_ref, arrived_ref, keys_hbm, values_hbm, out_ref,
                  keys_ref, values_ref, full, packed, sems):
    slots, cached, kv_width = keys_ref.shape
    rows = arrived_ref.shape[0]
    devices = rows // slots
    per_dev = query_cols // HD
    kv_cols = arrived_ref.shape[1] - query_cols
    pieces = HD // kv_cols
    share = HEADS // KVH
    scale = HD ** (-0.5)
    chunk = min(cached, CHUNK)
    widths = range(chunk, cached + 1, chunk)

    def longest(g):
        return len_ref[order_ref[g * group + group - 1]]

    def for_width(g, act):
        most = longest(g)
        for width in widths:
            pl.when((most > width - chunk) & (most <= width))(lambda width=width: act(width))

    def copies(g, i, width):
        at = g * group + i
        s = order_ref[at]
        for which, src, dst in ((0, keys_hbm, keys_ref), (1, values_hbm, values_ref)):
            cut = pl.ds(0, width)
            yield pltpu.make_async_copy(src.at[s, cut], dst.at[at, cut], sems.at[which, at])

    def begin(g, _):
        def start(width):
            for i in range(group):
                for copy in copies(g, i, width):
                    copy.start()

        for_width(g, start)
        return 0

    lax.fori_loop(0, slots // group, begin, 0)

    for i in range(per_dev):
        full[i] = arrived_ref[:, i * HD : (i + 1) * HD].astype(jnp.float32)
    target = lax.broadcasted_iota(jnp.int32, (rows, rows), 0)
    source = lax.broadcasted_iota(jnp.int32, (rows, rows), 1)
    holder = ((target // slots) * per_dev // share) * pieces
    fresh = arrived_ref[:, query_cols:]
    for which in range(2):
        for i in range(pieces):
            wanted = (which * (devices // 2) + holder + i) * slots + target % slots
            pick = (source == wanted).astype(jnp.bfloat16)
            full[per_dev + which, :, i * kv_cols : (i + 1) * kv_cols] = jnp.dot(
                pick, fresh, preferred_element_type=jnp.float32
            )
    row = lax.broadcasted_iota(jnp.int32, (HEADS, 1), 0)
    kv_head = ((row % devices) * per_dev + row // devices) // share
    lane_head = lax.broadcasted_iota(jnp.int32, (HEADS, kv_width), 1) // HD
    block_mask = lane_head == kv_head

    def of_slot(s, i):
        return full[i, pl.ds(s, devices, stride=slots), :]

    def repeated(s, i):
        return jnp.concatenate([of_slot(s, i)] * per_dev, axis=0)

    def one_group(g, _):
        def run(width):
            for i in range(group):
                for copy in copies(g, i, width):
                    copy.wait()
            ids = [order_ref[g * group + i] for i in range(group)]
            position = lax.broadcasted_iota(jnp.int32, (HEADS, width), 1)
            scores, owns = [], []
            for i, s in enumerate(ids):
                q = jnp.concatenate([of_slot(s, j) for j in range(per_dev)], axis=0)
                wide = jnp.where(block_mask, jnp.concatenate([q] * KVH, axis=1), 0.0)
                scores.append(
                    lax.dot_general(
                        wide.astype(jnp.bfloat16),
                        keys_ref[g * group + i, :width, :],
                        (((1,), (1,)), ((), ())),
                        preferred_element_type=jnp.float32,
                    )
                )
                owns.append(jnp.sum(q * repeated(s, per_dev), axis=1, keepdims=True) * scale)
            probs, weights = [], []
            for i, s in enumerate(ids):
                sc = jnp.where(position < len_ref[s], scores[i] * scale, -1e30)
                top = jnp.maximum(jnp.max(sc, axis=1, keepdims=True), owns[i])
                pr = jnp.exp(sc - top)
                own_prob = jnp.exp(owns[i] - top)
                total = jnp.sum(pr, axis=1, keepdims=True) + own_prob
                probs.append(pr.astype(jnp.bfloat16))
                weights.append((own_prob.astype(jnp.bfloat16).astype(jnp.float32), total))
            for i, s in enumerate(ids):
                all_heads = jnp.dot(
                    probs[i],
                    values_ref[g * group + i, :width, :],
                    preferred_element_type=jnp.float32,
                )
                mine = all_heads[:, :HD]
                for k in range(1, KVH):
                    mine = jnp.where(kv_head == k, all_heads[:, k * HD : (k + 1) * HD], mine)
                own_low, total = weights[i]
                mine = (mine + own_low * repeated(s, per_dev + 1)) / total
                for j in range(per_dev):
                    packed[j, pl.ds(s, devices, stride=slots), :] = mine[
                        j * devices : (j + 1) * devices
                    ]

        for_width(g, run)
        return 0

    lax.fori_loop(0, slots // group, one_group, 0)
    for i in range(per_dev):
        out_ref[:, i * HD : (i + 1) * HD] = packed[i].astype(jnp.bfloat16)


def attend(order, slot_len, arrived, key_cache, value_cache, query_cols):
    slots = key_cache.shape[0]
    rows = arrived.shape[0]
    group = max(g for g in range(1, GROUP + 1) if slots % g == 0)
    whole = pl.BlockSpec(memory_space=pltpu.VMEM)
    return pl.pallas_call(
        lambda *refs: attend_kernel(query_cols, group, *refs),
        in_specs=[pl.BlockSpec(memory_space=pltpu.SMEM)] * 2
        + [whole]
        + [pl.BlockSpec(memory_space=pl.ANY)] * 2,
        out_specs=whole,
        out_shape=jax.ShapeDtypeStruct((rows, query_cols), jnp.bfloat16),
        scratch_shapes=[
            pltpu.VMEM(key_cache.shape, key_cache.dtype),
            pltpu.VMEM(value_cache.shape, value_cache.dtype),
            pltpu.VMEM((query_cols // HD + 2, rows, HD), jnp.float32),
            pltpu.VMEM((query_cols // HD, rows, HD), jnp.float32),
            pltpu.SemaphoreType.DMA((2, slots)),
        ],
        compiler_params=pltpu.CompilerParams(vmem_limit_bytes=32 * MIB),
        name="attend",
    )(
        order,
        slot_len,
        arrived,
        pltpu.with_memory_space_constraint(key_cache, pltpu.HBM),
        pltpu.with_memory_space_constraint(value_cache, pltpu.HBM),
    )


def output_kernel(cuts, cols, fetching, slots_ref, back_ref, w_ref, *outs):
    requests = back_ref.shape[0]
    ids = lax.broadcasted_iota(jnp.int32, (requests, slots_ref.shape[1]), 0)
    order = (slots_ref[...] == ids).astype(jnp.bfloat16)
    starts = range(0, w_ref.shape[1], cols)
    copies = []
    if fetching:
        held, sems = outs[len(cuts)], outs[len(cuts) + 1]
        for i, start in enumerate(starts):
            cut = pl.ds(start, cols)
            copies.append(pltpu.make_async_copy(w_ref.at[:, cut], held.at[:, cut], sems.at[i]))
            copies[-1].start()
        w_ref = held
    rows = lax.dot_general(
        order, back_ref[...], (((0,), (0,)), ((), ())), preferred_element_type=jnp.float32
    ).astype(jnp.bfloat16)
    for i, start in enumerate(starts):
        cut = slice(start, start + cols)
        if fetching:
            copies[i].wait()
        out = jnp.dot(rows, w_ref[:, cut], preferred_element_type=jnp.float32).astype(jnp.bfloat16)
        first = 0
        for size, ref in zip(cuts, outs[: len(cuts)], strict=True):
            ref[:, cut] = out[first : first + size]
            first += size


def output(cuts, slots_local, returned, w_out, cols, fetching):
    model = w_out.shape[1]
    whole = pl.BlockSpec(memory_space=pltpu.VMEM)
    out_shape = [jax.ShapeDtypeStruct((size, model), jnp.bfloat16) for size in cuts]
    if fetching:
        out_shape.append(pltpu.VMEM(w_out.shape, w_out.dtype))
    place = pltpu.HBM if fetching else pltpu.VMEM
    return pl.pallas_call(
        lambda *refs: output_kernel(cuts, cols, fetching, *refs),
        in_specs=[whole] * 2 + [pl.BlockSpec(memory_space=pl.ANY) if fetching else whole],
        out_specs=[whole] * len(out_shape),
        out_shape=out_shape,
        scratch_shapes=[pltpu.SemaphoreType.DMA((model // cols,))] if fetching else [],
        compiler_params=pltpu.CompilerParams(vmem_limit_bytes=12 * MIB),
    )(slots_local, returned, pltpu.with_memory_space_constraint(w_out, place))


def add_up_kernel(starts, extra, block, *refs):
    outs = refs[2 * len(starts) + extra :]
    arrivals = refs[2 * len(starts) : 2 * len(starts) + extra]
    for i, (start, out) in enumerate(zip(starts, outs, strict=True)):
        cut = slice(start, start + block)
        total = refs[2 * i][cut, :].astype(jnp.float32) + refs[2 * i + 1][cut, :].astype(jnp.float32)
        for arrived in arrivals:
            total += arrived[...].astype(jnp.float32)
        out[...] = total.astype(jnp.bfloat16)


def add_up(pieces, arrivals, block):
    operands = [x for own, got, _ in pieces for x in (own, got)] + list(arrivals)
    starts = [start for _, _, start in pieces]
    model = operands[0].shape[1]
    whole = pl.BlockSpec(memory_space=pltpu.VMEM)
    return pl.pallas_call(
        lambda *refs: add_up_kernel(starts, len(arrivals), block, *refs),
        in_specs=[whole] * len(operands),
        out_specs=[whole] * len(starts),
        out_shape=[jax.ShapeDtypeStruct((block, model), jnp.bfloat16)] * len(starts),
        compiler_params=pltpu.CompilerParams(vmem_limit_bytes=8 * MIB),
    )(*operands)


def body(rows, norm_gain, w_query, w_keyval, w_out, key_cache, value_cache, lengths, slot_of):
    size = lax.axis_size("tensor")
    devices = lax.axis_size(AXES)
    half = size // 2
    block = rows.shape[0]
    slots_dev = key_cache.shape[0]
    query_cols = w_query.shape[1]
    forward = lambda x: lax.ppermute(x, AXES, ring_pairs(size))
    swap = lambda x: lax.ppermute(x, AXES, sibling_pairs(size))

    pool = lax.axis_index("pool")
    tensor = lax.axis_index("tensor")
    way = 1 - 2 * pool
    place = jnp.where(tensor % 2 == 0, tensor // 2, size - 1 - tensor // 2)

    def device_at(steps, owner):
        at = (place + way * steps + 2 * size) % size
        return owner * size + jnp.where(at < half, 2 * at, 2 * (size - 1 - at) + 1)

    slot_blocks = slot_of.reshape(devices, block)

    def slots_in(order):
        pick = jnp.stack(order)[:, None] == jnp.arange(devices, dtype=jnp.int32)[None, :]
        return jnp.sum(jnp.where(pick[:, :, None], slot_blocks[None], 0), axis=1).reshape(-1)

    order = [device_at(0, pool), device_at(0, 1 - pool)]
    late_order = []
    for k in range(1, half):
        order += [device_at(-k, pool), device_at(k, 1 - pool)]
        into = order if k < half - 1 else late_order
        into += [device_at(-k, 1 - pool), device_at(k, pool)]
    late_order += [device_at(-half, pool), device_at(half, 1 - pool)]
    own_slots = lax.axis_index(AXES) * slots_dev + jnp.arange(slots_dev, dtype=jnp.int32)
    slot_len = jnp.sum(
        jnp.where(slot_of[None, :] == own_slots[:, None], lengths[None, :], 0), axis=1
    )
    theirs, mine = [device_at(-half, 1 - pool)], [device_at(half, pool)]
    for k in range(half - 1, 0, -1):
        theirs += [device_at(-k, 1 - pool), device_at(-k, pool)]
        mine += [device_at(k, pool), device_at(k, 1 - pool)]
    theirs += [device_at(0, 1 - pool)]
    mine += [device_at(0, pool)]
    each = jnp.arange(slots_dev, dtype=jnp.int32)
    shorter = (slot_len[None, :] < slot_len[:, None]) | (
        (slot_len[None, :] == slot_len[:, None]) & (each[None, :] < each[:, None])
    )
    rank = jnp.sum(shorter.astype(jnp.int32), axis=1)
    by_length = jnp.sum(jnp.where(rank[None, :] == each[:, None], each[None, :], 0), axis=1)
    index = (
        slot_len,
        by_length,
        slots_in(order + late_order).reshape(1, -1),
        slots_in(theirs).reshape(1, -1),
        slots_in(mine[:3]).reshape(1, -1),
        slots_in(mine[3:]).reshape(1, -1),
    )

    normed = norm(rows, norm_gain)
    a, b = normed, swap(normed)
    b, index = lax.optimization_barrier((b, index))
    slot_len, by_length, slots_local, slots_theirs, slots_early, slots_rest = index
    blocks, late = [a, b], []
    for k in range(1, half):
        a, b = forward(a), forward(b)
        blocks += [a, swap(a)]
        into = blocks if k < half - 1 else late
        into += [b, swap(b)]
    a = forward(a)
    late += [a, swap(a)]

    part = w_query.shape[0] // PIECES
    pieces = [fetch(i * part, part, w_query, w_keyval) for i in range(PIECES)]
    early_rows = project(blocks, pieces)
    sending = project(late, pieces, slots_local, early_rows)
    arrived = lax.all_to_all(sending, AXES, split_axis=0, concat_axis=0, tiled=True)

    attended = attend(by_length, slot_len, arrived, key_cache, value_cache, query_cols)
    returned = lax.all_to_all(attended, AXES, split_axis=0, concat_axis=0, tiled=True)
    early = 3 * block
    rest = block * len(mine) - early
    cols = w_out.shape[1] // 8
    first, later, held = output((early, rest), slots_theirs, returned, w_out, cols, True)
    first, later = swap(first), swap(later)
    (own_first,) = output((early,), slots_early, returned, held, cols, False)
    (own_later,) = output((rest,), slots_rest, returned, held, cols, False)

    def chip_sum(items, arrivals=()):
        pieces = [(own_first, first, i) if i < 3 else (own_later, later, i - 3) for i in items]
        return add_up([(o, g, at * block) for o, g, at in pieces], arrivals, block)

    a, b = chip_sum((0, 2))
    a = forward(a)
    b = forward(b)
    at = 1
    for k in range(half - 1, 0, -1):
        (a,) = chip_sum((at,), (a,))
        a = forward(a)
        if k > 1:
            (b,) = chip_sum((at + 3,), (b,))
            b = forward(b)
        at += 2
    across = swap(b)
    (out,) = chip_sum((at,), (a, across))
    return out


def solution(mesh):
    placed = (
        P(("groups", "pool", "tensor"), None),
        P(),
        P(None, ("pool", "tensor")),
        P(None, ("pool", "tensor")),
        P(("pool", "tensor"), None),
        P(("groups", "pool", "tensor"), None, None),
        P(("groups", "pool", "tensor"), None, None),
        P("groups"),
        P("groups"),
    )

    return jax.shard_map(
        body,
        mesh=mesh,
        in_specs=placed,
        out_specs=P(("groups", "pool", "tensor"), None),
        check_vma=False,
    )
```
